512 devices in a mesh: sec: 32 (over z, y_lo), blk: 16 (over x, y_hi, core).
Axes of the slice: x: 4, y: 8 (y_hi: 2, y_lo: 4; y = y_hi * 4 + y_lo), z: 8, core: 2. Of those that a mesh axis runs over, the one named last changes fastest.
Arguments:
- wave: bfloat16 [32, 16, 256, 256], P('sec', 'blk'), may hold values from -6 to 6
- left_block_environment: bfloat16 [32, 16, 16, 256, 256], P('sec', 'blk'), may hold values from -0.375 to 0.375
- right_block_environment: bfloat16 [32, 16, 16, 256, 256], P('sec', 'blk'), may hold values from -0.09375 to 0.09375
- source_block: int32 [32, 16, 16], P('sec', 'blk'), may hold values from 0 to 15
- sector_size: int32 [32, 16], P('sec', 'blk'), may hold values from 1 to 256, 2560 in all within a row
Outputs:
- first_product: bfloat16 [32, 16, 256, 256], P('sec', 'blk')
- second_product: bfloat16 [32, 16, 256, 256], P('sec', 'blk')
The draws below stay inside these ranges and needn't reach their ends.
All inputs are finite; a program needn't handle non-finite values. No bound on the sum of `sector_size` on one device may be relied on, other than what follows from the above.
Results may differ from the reference program's by a relative error of at most 0.015.
Values may be sent and summed in bfloat16 or wider, within the bound.
No kernel may reach another device: no remote copies, remote signals or barrier semaphores. Data moves between devices by JAX's collectives and lax.ppermute only.
A program may use at most 64 MiB of HBM per device.

```python
import math
import jax
import jax.numpy as jnp
import numpy as np
from jax import lax

SB = 256
W = 16
BLK_DEV = 1
NB = 16
NSEC = 32
LIVE = 2560


def place_ends(result, own_key, least, top_value):
    spot = [jax.random.randint(jax.random.fold_in(own_key, axis), (), 0, length) for axis, length in enumerate(result.shape)]
    longest = result.shape.index(max(result.shape))
    beside = spot[:longest] + [(spot[longest] + 1) % result.shape[longest]] + spot[longest + 1:]
    return result.at[tuple(spot)].set(least).at[tuple(beside)].set(top_value)


def level_of(rng, extent, split, low, high):
    factor_of, own = 1.0, jax.random.fold_in(rng, 6)
    for axis_at, parts in split:
        draws = jnp.exp(jax.random.uniform(jax.random.fold_in(own, axis_at), (parts,), jnp.float32, low / len(split), high / len(split)))
        factor_of = factor_of * jnp.repeat(draws, extent[axis_at] // parts).reshape([-1 if axis == axis_at else 1 for axis in range(len(extent))])
    return factor_of


def split_up(number_of, total, limit, slope):
    portions = [(1 << 20) // math.isqrt(rank ** slope) + 1 for rank in range(2, number_of + 1)]
    spare, counts = total - limit - (number_of - 1), [1] * (number_of - 1)
    while spare > 0:
        candidates = [i for i in range(number_of - 1) if counts[i] < limit]
        whole, left = sum([portions[i] for i in candidates]), spare
        for i in candidates:
            extra = min(limit - counts[i], max(1, left * portions[i] // whole), spare)
            counts[i] = counts[i] + extra
            spare = spare - extra
    return np.array([limit] + counts)


def uneven_parts(stream_key, amount, total, bound, lean):
    if amount == 2:
        one = jax.random.randint(stream_key, (), max(1, total - bound), min(bound, total - 1) + 1)
        return jnp.stack([one, total - one])
    tallies = jnp.asarray(split_up(amount, total, bound, lean), jnp.int32)
    pairs = (amount - 1) // 2
    giver, taker = tallies[1:1 + 2 * pairs:2], tallies[2:2 + 2 * pairs:2]
    slack = jnp.minimum(giver - 1, bound - taker)
    moved = jax.random.randint(jax.random.fold_in(stream_key, 1), (pairs,), 0, 1 << 20) % (slack + 1)
    tallies = tallies.at[1:1 + 2 * pairs:2].set(giver - moved).at[2:2 + 2 * pairs:2].set(taker + moved)
    return tallies[jax.random.permutation(jax.random.fold_in(stream_key, 2), amount)]


def bell_draw(own_key, extent, width, limit, shards=(), held_as=jnp.bfloat16):
    loudness = level_of(own_key, extent, shards, -0.22, 0.18) if shards else 1.0
    values = jax.random.normal(own_key, extent, jnp.float32) * width * loudness
    return jnp.minimum(jnp.maximum(values, -limit), limit).astype(held_as)


def setup_inputs(seed: int = 0) -> dict:
    arg_keys = jax.random.split(jax.random.key(seed), 6)
    return {
        "wave": bell_draw(arg_keys[0], (NSEC, NB, SB, SB), 1.0, 6.0, ((0, 32), (1, 16))),
        "left_block_environment": bell_draw(arg_keys[1], (NSEC, NB, W, SB, SB), SB ** -0.5, 0.375, ((0, 32), (1, 16))),
        "right_block_environment": bell_draw(arg_keys[2], (NSEC, NB, W, SB, SB), (SB * W) ** -0.5, 0.09375, ((0, 32), (1, 16))),
        "source_block": place_ends(jax.random.randint(arg_keys[3], (NSEC, NB, W), 0, NB), jax.random.fold_in(arg_keys[3], 1), 0, NB - 1).astype(jnp.int32),
        "sector_size": jax.vmap(lambda own: uneven_parts(own, NB, LIVE, SB, 2))(jax.random.split(arg_keys[4], NSEC)).reshape((NSEC, NB)).astype(jnp.int32),
    }


def live_mask(sizes):
    rows = jnp.arange(SB, dtype=jnp.int32)
    first = rows[None, :, None] < sizes[:, None, None]
    second_apply = rows[None, None, :] < sizes[:, None, None]
    return (first & second_apply).astype(jnp.bfloat16)

def apply_section(left, pool, picks, right):
    chosen = pool[picks]
    inner = jnp.einsum('ktab,ktbc->ktac', left.astype(jnp.float32), chosen.astype(jnp.float32)).astype(jnp.bfloat16)
    return jnp.einsum('ktab,ktbc->kac', inner.astype(jnp.float32), right.astype(jnp.float32))

def phase_one(input_arrays):
    wave_s, left_s, right_s, picks, sizes = input_arrays
    mask = live_mask(sizes)
    live = wave_s * mask
    first = (apply_section(left_s, live, picks, right_s) * mask.astype(jnp.float32)).astype(jnp.bfloat16)
    first_f = first.astype(jnp.float32)
    squares = jnp.sum(first_f * first_f)
    count = jnp.sum((sizes * sizes).astype(jnp.float32))
    scale = lax.rsqrt(squares / count + 1e-06)
    trial_vector = (first_f * scale).astype(jnp.bfloat16)
    left_vector = jnp.einsum('ktab,kbc->ktac', left_s.astype(jnp.float32), trial_vector.astype(jnp.float32)).astype(jnp.bfloat16)
    terms = jnp.einsum('kba,ktbc->ktac', trial_vector.astype(jnp.float32), left_vector.astype(jnp.float32))
    grouped = terms.reshape(NB // BLK_DEV, BLK_DEV, W, SB, SB).sum(axis=1).astype(jnp.bfloat16)
    grouped = lax.optimization_barrier(grouped)
    total = grouped.astype(jnp.float32).sum(axis=0)
    factor = 1.0 / (SB * math.sqrt(NB))
    edge = (total * factor).astype(jnp.bfloat16)
    return (first, trial_vector, edge)

def phase_two(input_arrays):
    trial_vector, left_s, right_s, picks, sizes, incoming = input_arrays
    mask = live_mask(sizes)
    left_two = (left_s.astype(jnp.float32) + incoming[None].astype(jnp.float32)).astype(jnp.bfloat16)
    second_apply = apply_section(left_two, trial_vector, picks, right_s) * mask.astype(jnp.float32)
    return second_apply.astype(jnp.bfloat16)

def reference(wave, left_block_environment, right_block_environment, source_block, sector_size):
    first, trial_vector, edge = lax.map(phase_one, (wave, left_block_environment, right_block_environment, source_block, sector_size))
    incoming = jnp.concatenate([jnp.zeros_like(edge[:1]), edge[:-1]], axis=0)
    second_apply = lax.map(phase_two, (trial_vector, left_block_environment, right_block_environment, source_block, sector_size, incoming))
    return (first, second_apply)
```

```python
import math

import jax
import jax.numpy as jnp
from jax import lax
from jax.experimental import pallas as pl
from jax.experimental.pallas import tpu as pltpu
from jax.sharding import Mesh
from jax.sharding import PartitionSpec as P

BF = jnp.bfloat16
F32 = jnp.float32
TILE = 16
YROW = ("z", "yl", "yh")
SWAP = [(0, 1), (1, 0)]
VMEM = pl.BlockSpec(memory_space=pltpu.VMEM)
SMEM = pl.BlockSpec(memory_space=pltpu.SMEM)
ANY = pl.BlockSpec(memory_space=pl.ANY)
PARAMS = pltpu.CompilerParams(vmem_limit_bytes=24 << 20)


def dot(a, b):
    return jnp.dot(a, b, preferred_element_type=F32)


def pieces(value):
    high = value.astype(BF).astype(F32)
    mid = (value - high).astype(BF).astype(F32)
    return high, mid, value - high - mid


def pack(squares, count):
    width = squares.shape[-1]
    row = lax.broadcasted_iota(jnp.int32, (TILE, width), 0)
    tile = jnp.zeros((TILE, width), F32)
    for at, part in enumerate(pieces(squares) + pieces(count)):
        tile = jnp.where(row == at, jnp.broadcast_to(part, (TILE, width)), tile)
    return tile.astype(BF)


def unpack(tile):
    t = tile.astype(F32)
    return t[0:1] + t[1:2] + t[2:3], t[3:4] + t[4:5] + t[5:6]


def live(size, shape):
    rows = lax.broadcasted_iota(jnp.int32, shape, 0)
    columns = lax.broadcasted_iota(jnp.int32, shape, 1)
    return (rows < size) & (columns < size)


def place(source, meta, yh_known):
    x, yh, c = source // 4, (source // 2) % 2, source % 2
    other = lax.rem(c + meta[1], 2)
    if yh_known:
        yh = lax.rem(yh + meta[2], 2)
    return (other * 4 + x) * 2 + yh


def first_kernel(meta, picks, pool_own, pool_other, left_hbm, right_hbm,
                 first_out, message, stats, send, keep,
                 pool, left, right, inner, lv, pool_sem, left_sem, right_sem):
    channels, width = left.shape[0], left.shape[1]
    half = channels // 2
    pool_copies = [
        pltpu.make_async_copy(pool_own, pool.at[pl.ds(0, half)], pool_sem.at[0]),
        pltpu.make_async_copy(pool_other, pool.at[pl.ds(half, half)], pool_sem.at[1]),
    ]
    left_copies = [pltpu.make_async_copy(left_hbm.at[t], left.at[t], left_sem.at[t]) for t in range(channels)]
    right_copies = [pltpu.make_async_copy(right_hbm.at[t], right.at[t], right_sem.at[t]) for t in range(channels)]
    for copy in pool_copies + left_copies + right_copies:
        copy.start()
    for copy in pool_copies:
        copy.wait()
    for t in range(channels):
        left_copies[t].wait()
        block = pool[place(picks[t], meta, False)]
        inner[:, t * width:(t + 1) * width] = dot(left[t], block).astype(BF)
    for copy in right_copies:
        copy.wait()
    product = dot(inner[...], right[...].reshape(channels * width, width))
    size = meta[0]
    product = jnp.where(live(size, product.shape), product, 0.0).astype(BF)
    first_out[...] = product
    message[0:width, :] = product
    value = product.astype(F32)
    columns = jnp.sum(value * value, axis=0, keepdims=True)
    squares = jnp.broadcast_to(jnp.sum(columns, axis=1, keepdims=True), (1, width))
    count = jnp.full((1, width), size * size, jnp.int32).astype(F32)
    tile = pack(squares, count)
    message[width:width + TILE, :] = tile
    stats[...] = tile
    send[half * width:half * width + TILE, :] = tile
    turned = value.T.astype(BF)
    for t in range(channels):
        lv[t] = dot(left[t], product).astype(BF)
    mine = meta[1]
    for j in range(half):
        send[j * width:(j + 1) * width, :] = dot(turned, lv[(1 - mine) * half + j]).astype(BF)
    for j in range(half):
        keep[j * width:(j + 1) * width, :] = dot(turned, lv[mine * half + j]).astype(BF)


def core_sum_kernel(keep, stats, arrived, out):
    rows = keep.shape[0]
    quarter = rows // 4
    q0, c0 = unpack(stats[...])
    q1, c1 = unpack(arrived[rows:rows + TILE, :])
    tile = pack(q0 + q1, c0 + c1)
    for x in range(4):
        at = x * quarter
        out[x, 0:quarter, :] = (
            keep[at:at + quarter, :].astype(F32) + arrived[at:at + quarter, :].astype(F32)
        ).astype(BF)
        out[x, quarter:quarter + TILE, :] = tile


def row_sum_kernel(arrived, out):
    rows = out.shape[0] - TILE
    out[0:rows, :] = (
        (arrived[0, 0:rows, :].astype(F32) + arrived[1, 0:rows, :].astype(F32))
        + (arrived[2, 0:rows, :].astype(F32) + arrived[3, 0:rows, :].astype(F32))
    ).astype(BF)
    squares, count = unpack(arrived[0, rows:rows + TILE, :])
    for x in range(1, 4):
        q, c = unpack(arrived[x, rows:rows + TILE, :])
        squares, count = squares + q, count + c
    out[rows:rows + TILE, :] = pack(squares, count)


def edge_kernel(factor, near, far, out):
    rows = near.shape[0] - TILE
    q0, c0 = unpack(near[rows:rows + TILE, :])
    q1, c1 = unpack(far[rows:rows + TILE, :])
    weight = factor / ((q0 + q1) / jnp.maximum(c0 + c1, 1.0) + 1e-6)
    total = near[0:rows, :].astype(F32) + far[0:rows, :].astype(F32)
    edge = (total * weight).astype(BF)
    for x in range(4):
        out[x] = edge


def pool_two_kernel(meta, picks, own, other, left_hbm, right_hbm, g_out, base, pool, left, right, pool_sem, left_sem, right_sem):
    channels, width = left.shape[0], left.shape[1]
    pool_copies = [
        pltpu.make_async_copy(own, pool.at[pl.ds(0, 4)], pool_sem.at[0]),
        pltpu.make_async_copy(other, pool.at[pl.ds(4, 4)], pool_sem.at[1]),
    ]
    left_copies = [pltpu.make_async_copy(left_hbm.at[t], left.at[t], left_sem.at[t]) for t in range(channels)]
    right_copies = [pltpu.make_async_copy(right_hbm.at[t], right.at[t], right_sem.at[t]) for t in range(channels)]
    for copy in pool_copies + right_copies + left_copies:
        copy.start()
    for copy in pool_copies:
        copy.wait()
    squares = count = jnp.zeros((1, width), F32)
    span = width + TILE
    for at in range(8):
        for row in range(2):
            q, c = unpack(pool[at, row * span + width:(row + 1) * span, :])
            squares, count = squares + q, count + c
    scale = lax.rsqrt(squares / count + 1e-6)
    base[...] = jnp.zeros_like(base)
    for t in range(channels):
        right_copies[t].wait()
        left_copies[t].wait()
        slot = place(picks[t], meta, True)
        start = pl.multiple_of(lax.rem(slot, 2) * span, TILE)
        block = pool[slot // 2, pl.ds(start, width), :]
        g = (dot(block, right[t]) * scale).astype(BF)
        g_out[t] = g
        base[...] += dot(left[t], g)


def half_kernel(final, meta, edges, g, start, out):
    half, width = edges.shape[0] * 2, g.shape[1]
    side = meta[1] if not final else 1 - meta[1]
    total = start[...]
    for j in range(half):
        block = edges[j // 2, (j % 2) * width:(j % 2 + 1) * width, :]
        total = total + dot(block, g[side * half + j])
    if final:
        total = jnp.where(live(meta[0], total.shape), total, 0.0)
    out[...] = total.astype(out.dtype)


def call(kernel, shapes, specs, scratch, flops, moved):
    several = isinstance(shapes, (list, tuple))
    return pl.pallas_call(
        kernel,
        out_shape=[jax.ShapeDtypeStruct(*s) for s in shapes] if several else shapes,
        in_specs=specs,
        out_specs=[VMEM] * len(shapes) if several else VMEM,
        scratch_shapes=scratch,
        compiler_params=PARAMS,
        cost_estimate=pl.CostEstimate(flops=flops, bytes_accessed=moved, transcendentals=0),
    )


def one(shape, dtype):
    return jax.ShapeDtypeStruct(shape, dtype)


def for_each(value, count):
    return jnp.broadcast_to(value[None], (count, *value.shape))


def exchange(value, axes):
    return lax.all_to_all(value, axes, 0, 0, tiled=True)


def routes(z_count, y_count):
    def at(z, yl, yh):
        return (z * y_count + yl) * 2 + yh

    near, far = [], []
    for z in range(z_count):
        for yl in range(y_count):
            for yh in range(2):
                if yl + 1 < y_count:
                    following = (z, yl + 1, yh)
                elif z + 1 < z_count:
                    following = (z + 1, 0, 1 - yh)
                else:
                    continue
                near.append((at(z, yl, yh), at(*following)))
                far.append((at(z, yl, yh), at(following[0], following[1], 1 - following[2])))
    return near, far


def shards(wave, left_block_environment, right_block_environment, source_block, sector_size):
    left = left_block_environment[0, 0]
    right = right_block_environment[0, 0]
    picks = source_block[0, 0]
    size = sector_size[0, 0]
    channels, width = left.shape[0], left.shape[1]
    half = channels // 2
    span = width + TILE
    unit = 2 * channels * width**3
    block_bytes = width * width * 2
    meta = jnp.stack([size, lax.axis_index("c").astype(jnp.int32), lax.axis_index("yh").astype(jnp.int32)])

    masked = jnp.where(live(size, (width, width)), wave[0, 0], jnp.zeros((), BF))
    pool_own = exchange(for_each(masked, 8), ("x", "yh"))
    pool_other = lax.ppermute(pool_own, "c", SWAP)
    copies = [pltpu.SemaphoreType.DMA((2,)), pltpu.SemaphoreType.DMA((channels,)), pltpu.SemaphoreType.DMA((channels,))]
    stack = pltpu.VMEM((channels, width, width), BF)
    first, message, stats, send, keep = call(
        first_kernel,
        [((width, width), BF), ((span, width), BF), ((TILE, width), BF),
         ((half * width + TILE, width), BF), ((half * width, width), BF)],
        [SMEM, SMEM, ANY, ANY, ANY, ANY],
        [stack, stack, stack, pltpu.VMEM((width, channels * width), BF), stack, *copies],
        4 * unit, 5 * channels * block_bytes,
    )(meta, picks, pool_own, pool_other, left, right)

    arrived = lax.ppermute(send, "c", SWAP)
    message_other = lax.ppermute(message, "yh", SWAP)
    parts = call(
        core_sum_kernel, one((4, 2 * width + TILE, width), BF), [VMEM] * 3, [], 1 << 20, 3 * half * block_bytes
    )(keep, stats, arrived)
    parts = exchange(parts, "x")
    row = call(row_sum_kernel, one((2 * width + TILE, width), BF), [VMEM], [], 1 << 20, 10 * block_bytes)(parts)
    near, far = routes(lax.axis_size("z"), lax.axis_size("yl"))
    from_far = lax.ppermute(row, YROW, far)
    from_near = lax.ppermute(row, YROW, near)

    both = jnp.concatenate([message, message_other], axis=0)
    two_own = exchange(for_each(both, 4), "x")
    two_other = lax.ppermute(two_own, "c", SWAP)
    g, base = call(
        pool_two_kernel,
        [((channels, width, width), BF), ((width, width), F32)],
        [SMEM, SMEM, ANY, ANY, ANY, ANY],
        [pltpu.VMEM((8, 2 * span, width), BF), stack, stack, *copies],
        2 * unit, 5 * channels * block_bytes,
    )(meta, picks, two_own, two_other, left, right)

    factor = 1.0 / (width * math.sqrt(channels_of(sector_size)))
    edge = call(
        lambda *refs: edge_kernel(factor, *refs), one((4, 2 * width, width), BF), [VMEM] * 2, [], 1 << 20, 12 * block_bytes
    )(from_near, from_far)
    edges_own = exchange(edge, "x")
    edges_other = lax.ppermute(edges_own, "c", SWAP)
    partial = call(
        lambda *refs: half_kernel(False, *refs), one((width, width), F32), [SMEM, VMEM, VMEM, VMEM], [], unit // 2,
        3 * half * block_bytes,
    )(meta, edges_own, g, base)
    second = call(
        lambda *refs: half_kernel(True, *refs), one((width, width), BF), [SMEM, VMEM, VMEM, VMEM], [], unit // 2,
        3 * half * block_bytes,
    )(meta, edges_other, g, partial)
    return (first[None, None], second[None, None])


def channels_of(sector_size):
    return sector_size.shape[1] * lax.axis_size(("x", "yh", "c"))


def solution(mesh):
    finer = Mesh(mesh.devices.reshape(mesh.shape["sec"] // 4, 4, 4, 2, 2), ("z", "yl", "x", "yh", "c"))
    sec, blk = ("z", "yl"), ("x", "yh", "c")
    return jax.shard_map(
        shards,
        mesh=finer,
        in_specs=(
            P(sec, blk, None, None),
            P(sec, blk, None, None, None),
            P(sec, blk, None, None, None),
            P(sec, blk, None),
            P(sec, blk),
        ),
        out_specs=(P(sec, blk, None, None), P(sec, blk, None, None)),
        check_vma=False,
    )
```

```python
import math

import jax
import jax.numpy as jnp
from jax import lax
from jax.experimental import pallas as pl
from jax.experimental.pallas import tpu as pltpu
from jax.sharding import Mesh
from jax.sharding import PartitionSpec as P


BF = jnp.bfloat16
F32 = jnp.float32
TILE = 16
YROW = ("z", "yl", "yh")
SWAP = [(0, 1), (1, 0)]
VMEM = pl.BlockSpec(memory_space=pltpu.VMEM)
SMEM = pl.BlockSpec(memory_space=pltpu.SMEM)
ANY = pl.BlockSpec(memory_space=pl.ANY)
PARAMS = pltpu.CompilerParams(vmem_limit_bytes=16 << 20)


def dot(a, b):
    return jnp.dot(a, b, preferred_element_type=F32)


def pieces(value):
    high = value.astype(BF).astype(F32)
    mid = (value - high).astype(BF).astype(F32)
    return high, mid, value - high - mid


def pack(squares, count):
    width = squares.shape[-1]
    row = lax.broadcasted_iota(jnp.int32, (TILE, width), 0)
    tile = jnp.zeros((TILE, width), F32)
    for at, part in enumerate(pieces(squares) + pieces(count)):
        tile = jnp.where(row == at, jnp.broadcast_to(part, (TILE, width)), tile)
    return tile.astype(BF)


def unpack(tile):
    t = tile.astype(F32)
    return t[0:1] + t[1:2] + t[2:3], t[3:4] + t[4:5] + t[5:6]


def live(size, shape):
    rows = lax.broadcasted_iota(jnp.int32, shape, 0)
    columns = lax.broadcasted_iota(jnp.int32, shape, 1)
    return (rows < size) & (columns < size)


def place(source, meta):
    x, yh, c = source // 4, (source // 2) % 2, source % 2
    return lax.rem(c + meta[1], 2), lax.rem(yh + meta[2], 2), lax.rem(x + 4 - meta[3], 4)


def channel(meta, side, j):
    return side * 8 + lax.rem(meta[3] + j // 2, 4) * 2 + j % 2


def first_kernel(meta, picks, pool, left, right, first_out, message, stats, send, turned_out, inner, lv):
    channels, width = left.shape[0], left.shape[1]
    half = channels // 2
    for t in range(channels):
        c, yh, x = place(picks[t], meta)
        inner[:, t * width:(t + 1) * width] = dot(left[t], pool[(c * 2 + yh) * 4 + x]).astype(BF)
    product = dot(inner[...], right[...].reshape(channels * width, width))
    size = meta[0]
    product = jnp.where(live(size, product.shape), product, 0.0).astype(BF)
    first_out[...] = product
    message[0:width, :] = product
    value = product.astype(F32)
    columns = jnp.sum(value * value, axis=0, keepdims=True)
    squares = jnp.broadcast_to(jnp.sum(columns, axis=1, keepdims=True), (1, width))
    count = jnp.full((1, width), size * size, jnp.int32).astype(F32)
    tile = pack(squares, count)
    message[width:width + TILE, :] = tile
    stats[...] = tile
    send[half * width:half * width + TILE, :] = tile
    turned = value.T.astype(BF)
    turned_out[...] = turned
    for j in range(half):
        lv[j] = dot(left[channel(meta, 1 - meta[1], j)], product).astype(BF)
    for j in range(half):
        send[j * width:(j + 1) * width, :] = dot(turned, lv[j]).astype(BF)


def keep_kernel(meta, message, turned, left, keep, lv):
    half, width = left.shape[0] // 2, left.shape[1]
    first = message[0:width, :]
    for j in range(half):
        lv[j] = dot(left[channel(meta, meta[1], j)], first).astype(BF)
    for j in range(half):
        keep[j * width:(j + 1) * width, :] = dot(turned[...], lv[j]).astype(BF)


def core_sum_kernel(keep, stats, arrived, *outs):
    rows = keep.shape[0]
    quarter = rows // 4
    q0, c0 = unpack(stats[...])
    q1, c1 = unpack(arrived[rows:rows + TILE, :])
    tile = pack(q0 + q1, c0 + c1)
    for step, out in enumerate(outs):
        at = step * quarter
        out[0:quarter, :] = (
            keep[at:at + quarter, :].astype(F32) + arrived[at:at + quarter, :].astype(F32)
        ).astype(BF)
        out[quarter:quarter + TILE, :] = tile


def row_sum_kernel(a, b, c, d, out):
    rows = out.shape[0] - TILE
    out[0:rows, :] = (
        (a[0:rows, :].astype(F32) + b[0:rows, :].astype(F32)) + (c[0:rows, :].astype(F32) + d[0:rows, :].astype(F32))
    ).astype(BF)
    sums = [unpack(part[rows:rows + TILE, :]) for part in (a, b, c, d)]
    out[rows:rows + TILE, :] = pack(
        (sums[0][0] + sums[1][0]) + (sums[2][0] + sums[3][0]), (sums[0][1] + sums[1][1]) + (sums[2][1] + sums[3][1])
    )


def edge_kernel(factor, near, far, out):
    rows = near.shape[0] - TILE
    q0, c0 = unpack(near[rows:rows + TILE, :])
    q1, c1 = unpack(far[rows:rows + TILE, :])
    weight = factor / ((q0 + q1) / jnp.maximum(c0 + c1, 1.0) + 1e-6)
    total = near[0:rows, :].astype(F32) + far[0:rows, :].astype(F32)
    out[...] = (total * weight).astype(BF)


def pool_two_kernel(meta, picks, pool, left, right, g_out, base):
    channels, width = left.shape[0], left.shape[1]
    span = width + TILE
    squares = count = jnp.zeros((1, width), F32)
    for at in range(16):
        q, c = unpack(pool[at * span + width:(at + 1) * span, :])
        squares, count = squares + q, count + c
    scale = lax.rsqrt(squares / count + 1e-6)
    for t in range(channels):
        c, yh, x = place(picks[t], meta)
        start = pl.multiple_of(((c * 4 + x) * 2 + yh) * span, TILE)
        g_out[t] = (dot(pool[pl.ds(start, width), :], right[t]) * scale).astype(BF)
    total = dot(left[0], g_out[0])
    for t in range(1, channels):
        total = total + dot(left[t], g_out[t])
    base[...] = total


def half_kernel(final, meta, edges, g, start, out):
    width = g.shape[1]
    side = meta[1] if not final else 1 - meta[1]
    total = start[...]
    for j in range(edges.shape[0] // width):
        total = total + dot(edges[j * width:(j + 1) * width, :], g[channel(meta, side, j)])
    if final:
        total = jnp.where(live(meta[0], total.shape), total, 0.0)
    out[...] = total.astype(out.dtype)


def call(kernel, shapes, specs, scratch, flops, moved):
    several = isinstance(shapes, (list, tuple))
    return pl.pallas_call(
        kernel,
        out_shape=[jax.ShapeDtypeStruct(*s) for s in shapes] if several else shapes,
        in_specs=specs,
        out_specs=[VMEM] * len(shapes) if several else VMEM,
        scratch_shapes=scratch,
        compiler_params=PARAMS,
        cost_estimate=pl.CostEstimate(flops=flops, bytes_accessed=moved, transcendentals=0),
    )


def one(shape, dtype):
    return jax.ShapeDtypeStruct(shape, dtype)


def along_x(value, step):
    count = lax.axis_size("x")
    return lax.ppermute(value, "x", [(i, (i + step) % count) for i in range(count)])


def round_x(value):
    far = along_x(value, 2)
    return [value, along_x(value, 3), far, along_x(value, 1)]


def routes(z_count, y_count):
    def at(z, yl, yh):
        return (z * y_count + yl) * 2 + yh

    near, far = [], []
    for z in range(z_count):
        for yl in range(y_count):
            for yh in range(2):
                if yl + 1 < y_count:
                    following = (z, yl + 1, yh)
                elif z + 1 < z_count:
                    following = (z + 1, 0, 1 - yh)
                else:
                    continue
                near.append((at(z, yl, yh), at(*following)))
                far.append((at(z, yl, yh), at(following[0], following[1], 1 - following[2])))
    return near, far


def body(wave, left_block_environment, right_block_environment, source_block, sector_size):
    left = left_block_environment[0, 0]
    right = right_block_environment[0, 0]
    picks = source_block[0, 0]
    size = sector_size[0, 0]
    channels, width = left.shape[0], left.shape[1]
    half = channels // 2
    span = width + TILE
    unit = 2 * channels * width**3
    block_bytes = width * width * 2
    meta = jnp.stack([size, lax.axis_index("c").astype(jnp.int32), lax.axis_index("yh").astype(jnp.int32),
                      lax.axis_index("x").astype(jnp.int32)])

    masked = jnp.where(live(size, (width, width)), wave[0, 0], jnp.zeros((), BF))
    masked_other = lax.ppermute(masked, "yh", SWAP)
    own = jnp.stack(round_x(masked))
    across = lax.ppermute(own, "c", SWAP)
    own_other = jnp.stack(round_x(masked_other))
    across_other = lax.ppermute(own_other, "c", SWAP)
    pool = jnp.concatenate([own, own_other, across, across_other], axis=0)
    stack = pltpu.VMEM((half, width, width), BF)
    first, message, stats, send, turned = call(
        first_kernel,
        [((width, width), BF), ((span, width), BF), ((TILE, width), BF),
         ((half * width + TILE, width), BF), ((width, width), BF)],
        [SMEM, SMEM, VMEM, VMEM, VMEM],
        [pltpu.VMEM((width, channels * width), BF), stack],
        3 * unit, 4 * channels * block_bytes,
    )(meta, picks, pool, left, right)

    arrived = lax.ppermute(send, "c", SWAP)
    message_other = lax.ppermute(message, "yh", SWAP)
    keep = call(
        keep_kernel, one((half * width, width), BF), [SMEM, VMEM, VMEM, VMEM], [stack], unit, 2 * channels * block_bytes
    )(meta, message, turned, left)
    parts = call(
        core_sum_kernel, [((2 * width + TILE, width), BF)] * 4, [VMEM] * 3, [], 1 << 20, 3 * half * block_bytes
    )(keep, stats, arrived)
    arrived_x = [along_x(parts[2], 2), along_x(parts[1], 1), along_x(parts[3], 3)]
    row = call(
        row_sum_kernel, one((2 * width + TILE, width), BF), [VMEM] * 4, [], 1 << 20, 10 * block_bytes
    )(parts[0], *arrived_x)
    near, far = routes(lax.axis_size("z"), lax.axis_size("yl"))
    from_far = lax.ppermute(row, YROW, far)
    from_near = lax.ppermute(row, YROW, near)

    both = jnp.concatenate([message, message_other], axis=0)
    two_own = jnp.concatenate(round_x(both))
    two_other = lax.ppermute(two_own, "c", SWAP)
    pool_two = jnp.concatenate([two_own, two_other])
    g, base = call(
        pool_two_kernel,
        [((channels, width, width), BF), ((width, width), F32)],
        [SMEM, SMEM, VMEM, VMEM, VMEM],
        [],
        2 * unit, 4 * channels * block_bytes,
    )(meta, picks, pool_two, left, right)

    factor = 1.0 / (width * math.sqrt(channels_of(sector_size)))
    edge = call(
        lambda *refs: edge_kernel(factor, *refs), one((2 * width, width), BF), [VMEM] * 2, [], 1 << 20, 12 * block_bytes
    )(from_near, from_far)
    edges_own = jnp.concatenate(round_x(edge))
    edges_other = lax.ppermute(edges_own, "c", SWAP)
    partial = call(
        lambda *refs: half_kernel(False, *refs), one((width, width), F32), [SMEM, VMEM, VMEM, VMEM], [], unit // 2,
        3 * half * block_bytes,
    )(meta, edges_own, g, base)
    second = call(
        lambda *refs: half_kernel(True, *refs), one((width, width), BF), [SMEM, VMEM, VMEM, VMEM], [], unit // 2,
        3 * half * block_bytes,
    )(meta, edges_other, g, partial)
    return (first[None, None], second[None, None])


def channels_of(sector_size):
    return sector_size.shape[1] * lax.axis_size(("x", "yh", "c"))


def solution(mesh):
    finer = Mesh(mesh.devices.reshape(mesh.shape["sec"] // 4, 4, 4, 2, 2), ("z", "yl", "x", "yh", "c"))
    sec, blk = ("z", "yl"), ("x", "yh", "c")
    return jax.shard_map(
        body,
        mesh=finer,
        in_specs=(
            P(sec, blk, None, None),
            P(sec, blk, None, None, None),
            P(sec, blk, None, None, None),
            P(sec, blk, None),
            P(sec, blk),
        ),
        out_specs=(P(sec, blk, None, None), P(sec, blk, None, None)),
        check_vma=False,
    )
```

```python
import math

import jax
import jax.numpy as jnp
from jax import lax
from jax.experimental import pallas as pl
from jax.experimental.pallas import tpu as pltpu
from jax.sharding import Mesh
from jax.sharding import PartitionSpec as P


BF = jnp.bfloat16
F32 = jnp.float32
TILE = 16
UP = 128
YROW = ("z", "yl", "yh")
SWAP = [(0, 1), (1, 0)]
VMEM = pl.BlockSpec(memory_space=pltpu.VMEM)
SMEM = pl.BlockSpec(memory_space=pltpu.SMEM)
ANY = pl.BlockSpec(memory_space=pl.ANY)
PARAMS = pltpu.CompilerParams(vmem_limit_bytes=16 << 20)


def dot(a, b):
    return jnp.dot(a, b, preferred_element_type=F32)


def pieces(value):
    high = value.astype(BF).astype(F32)
    mid = (value - high).astype(BF).astype(F32)
    return high, mid, value - high - mid


def pack(squares, count):
    width = squares.shape[-1]
    row = lax.broadcasted_iota(jnp.int32, (TILE, width), 0)
    tile = jnp.zeros((TILE, width), F32)
    for at, part in enumerate(pieces(squares) + pieces(count)):
        tile = jnp.where(row == at, jnp.broadcast_to(part, (TILE, width)), tile)
    return tile.astype(BF)


def unpack(tile):
    t = tile.astype(F32)
    return t[0:1] + t[1:2] + t[2:3], t[3:4] + t[4:5] + t[5:6]


def live(size, shape):
    rows = lax.broadcasted_iota(jnp.int32, shape, 0)
    columns = lax.broadcasted_iota(jnp.int32, shape, 1)
    return (rows < size) & (columns < size)


def place(source, meta):
    x, yh, c = source // 4, (source // 2) % 2, source % 2
    return lax.rem(c + meta[1], 2), lax.rem(yh + meta[2], 2), lax.rem(x + 4 - meta[3], 4)


def channel(meta, side, j):
    return side * 8 + lax.rem(meta[3] + j // 2, 4) * 2 + j % 2


def first_kernel(meta, picks, pool, left, right, first_out, message, stats, send, turned_out, inner, lv):
    channels, width = left.shape[0], left.shape[1]
    half = channels // 2
    for t in range(channels):
        c, yh, x = place(picks[t], meta)
        inner[:, t * width:(t + 1) * width] = dot(left[t], pool[(c * 2 + yh) * 4 + x]).astype(BF)
    product = dot(inner[...], right[...].reshape(channels * width, width))
    size = meta[0]
    product = jnp.where(live(size, product.shape), product, 0.0).astype(BF)
    first_out[...] = product
    message[0:width, :] = product
    value = product.astype(F32)
    columns = jnp.sum(value * value, axis=0, keepdims=True)
    squares = jnp.broadcast_to(jnp.sum(columns, axis=1, keepdims=True), (1, width))
    count = jnp.full((1, width), size * size, jnp.int32).astype(F32)
    tile = pack(squares, count)
    message[width:width + TILE, :] = tile
    stats[...] = tile
    send[half * width:half * width + TILE, :] = tile
    turned = value.T.astype(BF)
    turned_out[...] = turned
    for j in range(half):
        lv[j] = dot(left[channel(meta, 1 - meta[1], j)], product).astype(BF)
    for j in range(half):
        send[j * width:(j + 1) * width, :] = dot(turned, lv[j]).astype(BF)


def keep_kernel(meta, message, turned, left, keep, lv):
    half, width = left.shape[0] // 2, left.shape[1]
    first = message[0:width, :]
    for j in range(half):
        lv[j] = dot(left[channel(meta, meta[1], j)], first).astype(BF)
    for j in range(half):
        keep[j * width:(j + 1) * width, :] = dot(turned[...], lv[j]).astype(BF)


def core_sum_kernel(keep, stats, arrived, *outs):
    rows = keep.shape[0]
    quarter = rows // 4
    q0, c0 = unpack(stats[...])
    q1, c1 = unpack(arrived[rows:rows + TILE, :])
    tile = pack(q0 + q1, c0 + c1)
    for step, out in enumerate(outs):
        at = step * quarter
        out[0:quarter, :] = (
            keep[at:at + quarter, :].astype(F32) + arrived[at:at + quarter, :].astype(F32)
        ).astype(BF)
        out[quarter:quarter + TILE, :] = tile


def row_sum_kernel(a, b, c, d, out):
    rows = out.shape[0] - TILE
    out[0:rows, :] = (
        (a[0:rows, :].astype(F32) + b[0:rows, :].astype(F32)) + (c[0:rows, :].astype(F32) + d[0:rows, :].astype(F32))
    ).astype(BF)
    sums = [unpack(part[rows:rows + TILE, :]) for part in (a, b, c, d)]
    out[rows:rows + TILE, :] = pack(
        (sums[0][0] + sums[1][0]) + (sums[2][0] + sums[3][0]), (sums[0][1] + sums[1][1]) + (sums[2][1] + sums[3][1])
    )


def edge_kernel(factor, near, far_up, far, out):
    rows = near.shape[0] - TILE
    up = far_up.shape[0]
    q0, c0 = unpack(near[rows:rows + TILE, :])
    q1, c1 = unpack(far[rows - up:rows - up + TILE, :])
    weight = factor / ((q0 + q1) / jnp.maximum(c0 + c1, 1.0) + 1e-6)
    out[0:up, :] = ((near[0:up, :].astype(F32) + far_up[...].astype(F32)) * weight).astype(BF)
    out[up:rows, :] = ((near[up:rows, :].astype(F32) + far[0:rows - up, :].astype(F32)) * weight).astype(BF)


def pool_two_kernel(meta, picks, pool, left, right, g_out, base):
    channels, width = left.shape[0], left.shape[1]
    span = width + TILE
    squares = count = jnp.zeros((1, width), F32)
    for at in range(16):
        q, c = unpack(pool[at * span + width:(at + 1) * span, :])
        squares, count = squares + q, count + c
    scale = lax.rsqrt(squares / count + 1e-6)
    for t in range(channels):
        c, yh, x = place(picks[t], meta)
        start = pl.multiple_of(((c * 4 + x) * 2 + yh) * span, TILE)
        g_out[t] = (dot(pool[pl.ds(start, width), :], right[t]) * scale).astype(BF)
    total = dot(left[0], g_out[0])
    for t in range(1, channels):
        total = total + dot(left[t], g_out[t])
    base[...] = total


def half_kernel(final, meta, edges, g, start, out):
    width = g.shape[1]
    side = meta[1] if not final else 1 - meta[1]
    total = start[...]
    for j in range(edges.shape[0] // width):
        total = total + dot(edges[j * width:(j + 1) * width, :], g[channel(meta, side, j)])
    if final:
        total = jnp.where(live(meta[0], total.shape), total, 0.0)
    out[...] = total.astype(out.dtype)


def call(kernel, shapes, specs, scratch, flops, moved):
    several = isinstance(shapes, (list, tuple))
    return pl.pallas_call(
        kernel,
        out_shape=[jax.ShapeDtypeStruct(*s) for s in shapes] if several else shapes,
        in_specs=specs,
        out_specs=[VMEM] * len(shapes) if several else VMEM,
        scratch_shapes=scratch,
        compiler_params=PARAMS,
        cost_estimate=pl.CostEstimate(flops=flops, bytes_accessed=moved, transcendentals=0),
    )


def one(shape, dtype):
    return jax.ShapeDtypeStruct(shape, dtype)


def along_x(value, step):
    count = lax.axis_size("x")
    return lax.ppermute(value, "x", [(i, (i + step) % count) for i in range(count)])


def round_x(value):
    far = along_x(value, 2)
    return [value, along_x(value, 3), far, along_x(value, 1)]


def routes(z_count):
    near, far, up_two, up_three = [], [], [], []

    def at(z, y):
        return (z * 4 + y % 4) * 2 + (y // 4) % 2

    for z in range(z_count):
        for y in range(8):
            up_two.append((at(z, y), at(z, y + 2)))
            next_z = z + (y % 4 == 3)
            if next_z < z_count:
                near.append((at(z, y), at(next_z, y + 1)))
                far.append((at(z, y), at(next_z, y + 5)))
                up_three.append((at(z, y + 2), at(next_z, y + 5)))
    return near, far, up_two, up_three


def body(wave, left_block_environment, right_block_environment, source_block, sector_size):
    left = left_block_environment[0, 0]
    right = right_block_environment[0, 0]
    picks = source_block[0, 0]
    size = sector_size[0, 0]
    channels, width = left.shape[0], left.shape[1]
    half = channels // 2
    span = width + TILE
    unit = 2 * channels * width**3
    block_bytes = width * width * 2
    meta = jnp.stack([size, *(lax.axis_index(axis).astype(jnp.int32) for axis in ("c", "yh", "x"))])

    masked = jnp.where(live(size, (width, width)), wave[0, 0], jnp.zeros((), BF))
    masked_other = lax.ppermute(masked, "yh", SWAP)
    own = jnp.stack(round_x(masked))
    across = lax.ppermute(own, "c", SWAP)
    diagonal = lax.ppermute(masked, ("x", "yh"), [(2 * x + y, 2 * ((x + 2) % 4) + 1 - y) for x in range(4) for y in range(2)])
    own_other = jnp.stack([masked_other, along_x(masked_other, 3), diagonal, along_x(masked_other, 1)])
    across_other = lax.ppermute(own_other, "c", SWAP)
    pool = jnp.concatenate([own, own_other, across, across_other], axis=0)
    stack = pltpu.VMEM((half, width, width), BF)
    first, message, stats, send, turned = call(
        first_kernel,
        [((width, width), BF), ((span, width), BF), ((TILE, width), BF),
         ((half * width + TILE, width), BF), ((width, width), BF)],
        [SMEM, SMEM, VMEM, VMEM, VMEM],
        [pltpu.VMEM((width, channels * width), BF), stack],
        3 * unit, 4 * channels * block_bytes,
    )(meta, picks, pool, left, right)

    arrived = lax.ppermute(send, "c", SWAP)
    message_other = lax.ppermute(message, "yh", SWAP)
    keep = call(
        keep_kernel, one((half * width, width), BF), [SMEM, VMEM, VMEM, VMEM], [stack], unit, 2 * channels * block_bytes
    )(meta, message, turned, left)
    parts = call(
        core_sum_kernel, [((2 * width + TILE, width), BF)] * 4, [VMEM] * 3, [], 1 << 20, 3 * half * block_bytes
    )(keep, stats, arrived)
    arrived_x = [along_x(parts[2], 2), along_x(parts[1], 1), along_x(parts[3], 3)]
    row = call(
        row_sum_kernel, one((2 * width + TILE, width), BF), [VMEM] * 4, [], 1 << 20, 10 * block_bytes
    )(parts[0], *arrived_x)
    near, far, up_two, up_three = routes(lax.axis_size("z"))
    passing = lax.ppermute(row[0:UP], YROW, up_two)
    from_far = lax.ppermute(row[UP:], YROW, far)
    from_near = lax.ppermute(row, YROW, near)
    from_far_up = lax.ppermute(passing, YROW, up_three)

    both = jnp.concatenate([message, message_other], axis=0)
    two_own = jnp.concatenate(round_x(both))
    two_other = lax.ppermute(two_own, "c", SWAP)
    pool_two = jnp.concatenate([two_own, two_other])
    g, base = call(
        pool_two_kernel,
        [((channels, width, width), BF), ((width, width), F32)],
        [SMEM, SMEM, VMEM, VMEM, VMEM],
        [],
        2 * unit, 4 * channels * block_bytes,
    )(meta, picks, pool_two, left, right)

    factor = 1.0 / (width * math.sqrt(channels_of(sector_size)))
    edge = call(
        lambda *refs: edge_kernel(factor, *refs), one((2 * width, width), BF), [VMEM] * 3, [], 1 << 20, 12 * block_bytes
    )(from_near, from_far_up, from_far)
    edges_own = jnp.concatenate(round_x(edge))
    edges_other = lax.ppermute(edges_own, "c", SWAP)
    partial = call(
        lambda *refs: half_kernel(False, *refs), one((width, width), F32), [SMEM, VMEM, VMEM, VMEM], [], unit // 2,
        3 * half * block_bytes,
    )(meta, edges_own, g, base)
    second = call(
        lambda *refs: half_kernel(True, *refs), one((width, width), BF), [SMEM, VMEM, VMEM, VMEM], [], unit // 2,
        3 * half * block_bytes,
    )(meta, edges_other, g, partial)
    return (first[None, None], second[None, None])


def channels_of(sector_size):
    return sector_size.shape[1] * lax.axis_size(("x", "yh", "c"))


def solution(mesh):
    finer = Mesh(mesh.devices.reshape(mesh.shape["sec"] // 4, 4, 4, 2, 2), ("z", "yl", "x", "yh", "c"))
    sec, blk = ("z", "yl"), ("x", "yh", "c")
    return jax.shard_map(
        body,
        mesh=finer,
        in_specs=(
            P(sec, blk, None, None),
            P(sec, blk, None, None, None),
            P(sec, blk, None, None, None),
            P(sec, blk, None),
            P(sec, blk),
        ),
        out_specs=(P(sec, blk, None, None), P(sec, blk, None, None)),
        check_vma=False,
    )
```

```python
import math

import jax
import jax.numpy as jnp
from jax import lax
from jax.experimental import pallas as pl
from jax.experimental.pallas import tpu as pltpu
from jax.sharding import Mesh
from jax.sharding import PartitionSpec as P


BF = jnp.bfloat16
F32 = jnp.float32
TILE = 16
YROW = ("z", "yl", "yh")
SWAP = [(0, 1), (1, 0)]
VMEM = pl.BlockSpec(memory_space=pltpu.VMEM)
SMEM = pl.BlockSpec(memory_space=pltpu.SMEM)
ANY = pl.BlockSpec(memory_space=pl.ANY)
PARAMS = pltpu.CompilerParams(vmem_limit_bytes=16 << 20)


def dot(a, b):
    return jnp.dot(a, b, preferred_element_type=F32)


def pieces(value):
    high = value.astype(BF).astype(F32)
    mid = (value - high).astype(BF).astype(F32)
    return high, mid, value - high - mid


def pack(squares, count):
    width = squares.shape[-1]
    row = lax.broadcasted_iota(jnp.int32, (TILE, width), 0)
    tile = jnp.zeros((TILE, width), F32)
    for at, part in enumerate(pieces(squares) + pieces(count)):
        tile = jnp.where(row == at, jnp.broadcast_to(part, (TILE, width)), tile)
    return tile.astype(BF)


def unpack(tile):
    t = tile.astype(F32)
    return t[0:1] + t[1:2] + t[2:3], t[3:4] + t[4:5] + t[5:6]


def live(size, shape):
    rows = lax.broadcasted_iota(jnp.int32, shape, 0)
    columns = lax.broadcasted_iota(jnp.int32, shape, 1)
    return (rows < size) & (columns < size)


def place(source, meta):
    x, yh, c = source // 4, (source // 2) % 2, source % 2
    return lax.rem(c + meta[1], 2), lax.rem(yh + meta[2], 2), lax.rem(x + 4 - meta[3], 4)


def channel(meta, side, j):
    return side * 8 + lax.rem(meta[3] + j // 2, 4) * 2 + j % 2


def first_kernel(meta, picks, pool, left, right, message, inner):
    channels, width = left.shape[0], left.shape[1]
    for t in range(channels):
        c, yh, step = place(picks[t], meta)
        inner[:, t * width:(t + 1) * width] = dot(left[t], pool[(c * 2 + yh) * 4 + step]).astype(BF)
    product = dot(inner[...], right[...].reshape(channels * width, width))
    size = meta[0]
    product = jnp.where(live(size, product.shape), product, 0.0).astype(BF)
    message[0:width, :] = product
    value = product.astype(F32)
    columns = jnp.sum(value * value, axis=0, keepdims=True)
    squares = jnp.broadcast_to(jnp.sum(columns, axis=1, keepdims=True), (1, width))
    count = jnp.full((1, width), size * size, jnp.int32).astype(F32)
    message[width:width + TILE, :] = pack(squares, count)


def terms(message, left_of, lv, count):
    width = message.shape[1]
    first = message[0:width, :]
    turned = first.astype(F32).T.astype(BF)
    for j in range(count):
        lv[j] = dot(left_of(j), first).astype(BF)
    return [lambda j=j: dot(turned, lv[j]) for j in range(count)]


def keep_kernel(meta, message, left, keep, lv):
    half = left.shape[0] // 2
    for j, term in enumerate(terms(message, lambda j: left[channel(meta, meta[1], j)], lv, half)):
        keep[j] = term()


def core_sum_kernel(meta, message, keep, left, *refs):
    own, lv, outs = refs[0], refs[-1], refs[1:-1]
    half, width = left.shape[0], left.shape[1]
    q0, c0 = unpack(own[width:width + TILE, :])
    q1, c1 = unpack(message[width:width + TILE, :])
    tile = pack(q0 + q1, c0 + c1)
    for out in outs:
        out[2 * width:2 * width + TILE, :] = tile
    for j, term in enumerate(terms(message, lambda j: left[channel(meta, 0, j)], lv, half)):
        outs[j // 2][(j % 2) * width:(j % 2 + 1) * width, :] = (keep[j] + term()).astype(BF)


def row_sum_kernel(a, b, c, d, out):
    rows = out.shape[0] - TILE
    out[0:rows, :] = (
        (a[0:rows, :].astype(F32) + b[0:rows, :].astype(F32)) + (c[0:rows, :].astype(F32) + d[0:rows, :].astype(F32))
    ).astype(BF)
    sums = [unpack(part[rows:rows + TILE, :]) for part in (a, b, c, d)]
    out[rows:rows + TILE, :] = pack(
        (sums[0][0] + sums[1][0]) + (sums[2][0] + sums[3][0]), (sums[0][1] + sums[1][1]) + (sums[2][1] + sums[3][1])
    )


def edge_kernel(factor, near, far, out):
    rows = near.shape[0] - TILE
    q0, c0 = unpack(near[rows:rows + TILE, :])
    q1, c1 = unpack(far[rows:rows + TILE, :])
    weight = factor / ((q0 + q1) / jnp.maximum(c0 + c1, 1.0) + 1e-6)
    total = near[0:rows, :].astype(F32) + far[0:rows, :].astype(F32)
    out[...] = (total * weight).astype(BF)


def pool_two_kernel(meta, picks, pool, left, right, g_own, g_send, base, g):
    channels, width = left.shape[0], left.shape[1]
    half = channels // 2
    span = width + TILE
    squares = count = jnp.zeros((1, width), F32)
    for at in range(16):
        q, c = unpack(pool[at * span + width:(at + 1) * span, :])
        squares, count = squares + q, count + c
    scale = lax.rsqrt(squares / count + 1e-6)
    for j in range(channels):
        t = channel(meta, lax.rem(meta[1] + j // half, 2), j % half)
        c, yh, step = place(picks[t], meta)
        start = pl.multiple_of(((c * 4 + step) * 2 + yh) * span, TILE)
        block = (dot(pool[pl.ds(start, width), :], right[t]) * scale).astype(BF)
        (g_own if j < half else g_send)[j % half] = block
        g[j] = left[t]
    total = dot(g[0], g_own[0])
    for j in range(1, half):
        total = total + dot(g[j], g_own[j])
    for j in range(half):
        total = total + dot(g[half + j], g_send[j])
    base[...] = total


def other_kernel(edges, g, out):
    width = g.shape[1]
    total = dot(edges[0:width, :], g[0])
    for j in range(1, g.shape[0]):
        total = total + dot(edges[j * width:(j + 1) * width, :], g[j])
    out[...] = total


def own_kernel(edges, g, base, out):
    width = g.shape[1]
    total = base[...]
    for j in range(g.shape[0]):
        total = total + dot(edges[j * width:(j + 1) * width, :], g[j])
    out[...] = total


def second_kernel(meta, own, other, out):
    total = own[...] + other[...]
    out[...] = jnp.where(live(meta[0], total.shape), total, 0.0).astype(out.dtype)


def call(kernel, shapes, specs, scratch, flops, moved):
    several = isinstance(shapes, (list, tuple))
    return pl.pallas_call(
        kernel,
        out_shape=[jax.ShapeDtypeStruct(*s) for s in shapes] if several else shapes,
        in_specs=specs,
        out_specs=[VMEM] * len(shapes) if several else VMEM,
        scratch_shapes=scratch,
        compiler_params=PARAMS,
        cost_estimate=pl.CostEstimate(flops=flops, bytes_accessed=moved, transcendentals=0),
    )


def one(shape, dtype):
    return jax.ShapeDtypeStruct(shape, dtype)


def along_x(value, step):
    count = lax.axis_size("x")
    return lax.ppermute(value, "x", [(i, (i + step) % count) for i in range(count)])


def round_x(value):
    far = along_x(value, 2)
    return [value, along_x(value, 3), far, along_x(value, 1)]


def routes(z_count, y_count):
    def at(z, yl, yh):
        return (z * y_count + yl) * 2 + yh

    near, far = [], []
    for z in range(z_count):
        for yl in range(y_count):
            for yh in range(2):
                if yl + 1 < y_count:
                    following = (z, yl + 1, yh)
                elif z + 1 < z_count:
                    following = (z + 1, 0, 1 - yh)
                else:
                    continue
                near.append((at(z, yl, yh), at(*following)))
                far.append((at(z, yl, yh), at(following[0], following[1], 1 - following[2])))
    return near, far


def body(wave, left_block_environment, right_block_environment, source_block, sector_size):
    left = left_block_environment[0, 0]
    right = right_block_environment[0, 0]
    picks = source_block[0, 0]
    size = sector_size[0, 0]
    channels, width = left.shape[0], left.shape[1]
    half = channels // 2
    span = width + TILE
    unit = 2 * channels * width**3
    block_bytes = width * width * 2
    meta = jnp.stack([size, *(lax.axis_index(axis).astype(jnp.int32) for axis in ("c", "yh", "x"))])

    masked = jnp.where(live(size, (width, width)), wave[0, 0], jnp.zeros((), BF))
    masked_other = lax.ppermute(masked, "yh", SWAP)
    own = jnp.stack(round_x(masked))
    left_send = lax.dynamic_slice_in_dim(left, (1 - lax.axis_index("c")) * half, half)
    left_other = lax.ppermute(left_send, "c", SWAP)
    across = lax.ppermute(own, "c", SWAP)
    own_other = jnp.stack(round_x(masked_other))
    across_other = lax.ppermute(own_other, "c", SWAP)
    pool = jnp.concatenate([own, own_other, across, across_other], axis=0)
    stack = pltpu.VMEM((half, width, width), BF)
    message = call(
        first_kernel, one((span, width), BF), [SMEM, SMEM, VMEM, VMEM, VMEM],
        [pltpu.VMEM((width, channels * width), BF)], 2 * unit, 4 * channels * block_bytes,
    )(meta, picks, pool, left, right)
    first = message[0:width]

    message_core = lax.ppermute(message, "c", SWAP)
    message_other = lax.ppermute(message, "yh", SWAP)
    keep = call(
        keep_kernel, one((half, width, width), F32), [SMEM, VMEM, VMEM], [stack], unit, 2 * channels * block_bytes
    )(meta, message, left)
    parts = call(
        core_sum_kernel, [((2 * width + TILE, width), BF)] * 4, [SMEM] + [VMEM] * 4, [stack], unit, 3 * half * block_bytes
    )(meta, message_core, keep, left_other, message)
    arrived_x = [along_x(parts[2], 2), along_x(parts[1], 1), along_x(parts[3], 3)]
    row = call(
        row_sum_kernel, one((2 * width + TILE, width), BF), [VMEM] * 4, [], 1 << 20, 10 * block_bytes
    )(parts[0], *arrived_x)
    near, far = routes(lax.axis_size("z"), lax.axis_size("yl"))
    from_far = lax.ppermute(row, YROW, far)
    from_near = lax.ppermute(row, YROW, near)

    both = jnp.concatenate([message, message_other], axis=0)
    two_own = jnp.concatenate(round_x(both))
    two_other = lax.ppermute(two_own, "c", SWAP)
    pool_two = jnp.concatenate([two_own, two_other])
    g_own, g_send, base = call(
        pool_two_kernel,
        [((half, width, width), BF), ((half, width, width), BF), ((width, width), F32)],
        [SMEM, SMEM, VMEM, VMEM, VMEM],
        [pltpu.VMEM((channels, width, width), BF)],
        2 * unit, 4 * channels * block_bytes,
    )(meta, picks, pool_two, left, right)
    g_other = lax.ppermute(g_send, "c", SWAP)

    factor = 1.0 / (width * math.sqrt(channels_of(sector_size)))
    edge = call(
        lambda *refs: edge_kernel(factor, *refs), one((2 * width, width), BF), [VMEM] * 2, [], 1 << 20, 12 * block_bytes
    )(from_near, from_far)
    edges_own = jnp.concatenate(round_x(edge))
    for_other = call(other_kernel, one((width, width), F32), [VMEM] * 2, [], unit // 2, 3 * half * block_bytes)(
        edges_own, g_other
    )
    from_other = lax.ppermute(for_other, "c", SWAP)
    from_own = call(own_kernel, one((width, width), F32), [VMEM] * 3, [], unit // 2, 3 * half * block_bytes)(
        edges_own, g_own, base
    )
    second = call(second_kernel, one((width, width), BF), [SMEM, VMEM, VMEM], [], 1 << 18, 3 * block_bytes)(
        meta, from_own, from_other
    )
    return (first[None, None], second[None, None])


def channels_of(sector_size):
    return sector_size.shape[1] * lax.axis_size(("x", "yh", "c"))


def solution(mesh):
    finer = Mesh(mesh.devices.reshape(mesh.shape["sec"] // 4, 4, 4, 2, 2), ("z", "yl", "x", "yh", "c"))
    sec, blk = ("z", "yl"), ("x", "yh", "c")
    return jax.shard_map(
        body,
        mesh=finer,
        in_specs=(
            P(sec, blk, None, None),
            P(sec, blk, None, None, None),
            P(sec, blk, None, None, None),
            P(sec, blk, None),
            P(sec, blk),
        ),
        out_specs=(P(sec, blk, None, None), P(sec, blk, None, None)),
        check_vma=False,
    )
```

```python
import math

import jax
import jax.numpy as jnp
from jax import lax
from jax.experimental import pallas as pl
from jax.experimental.pallas import tpu as pltpu
from jax.sharding import Mesh
from jax.sharding import PartitionSpec as P


BF = jnp.bfloat16
F32 = jnp.float32
TILE = 8
YROW = ("z", "yl", "yh")
SWAP = [(0, 1), (1, 0)]
VMEM = pl.BlockSpec(memory_space=pltpu.VMEM)
SMEM = pl.BlockSpec(memory_space=pltpu.SMEM)
ANY = pl.BlockSpec(memory_space=pl.ANY)
PARAMS = pltpu.CompilerParams(vmem_limit_bytes=16 << 20)


def dot(a, b):
    return jnp.dot(a, b, preferred_element_type=F32)


def pieces(value):
    high = value.astype(BF).astype(F32)
    mid = (value - high).astype(BF).astype(F32)
    return high, mid, value - high - mid


def pack(squares, count):
    width = squares.shape[-1]
    row = lax.broadcasted_iota(jnp.int32, (TILE, width), 0)
    tile = jnp.zeros((TILE, width), F32)
    for at, part in enumerate(pieces(squares) + pieces(count)):
        tile = jnp.where(row == at, jnp.broadcast_to(part, (TILE, width)), tile)
    return tile.astype(BF)


def unpack(tile):
    t = tile.astype(F32)
    return t[0:1] + t[1:2] + t[2:3], t[3:4] + t[4:5] + t[5:6]


def live(size, shape):
    rows = lax.broadcasted_iota(jnp.int32, shape, 0)
    columns = lax.broadcasted_iota(jnp.int32, shape, 1)
    return (rows < size) & (columns < size)


def place(source, meta):
    x, yh, c = source // 4, (source // 2) % 2, source % 2
    return lax.rem(c + meta[1], 2), lax.rem(yh + meta[2], 2), lax.rem(x + 4 - meta[3], 4)


def channel(meta, side, j):
    return side * 8 + lax.rem(meta[3] + j // 2, 4) * 2 + j % 2


def first_kernel(meta, picks, pool, left, right, first_out, message, stats, send, turned_out, inner, lv):
    channels, width = left.shape[0], left.shape[1]
    half = channels // 2
    for t in range(channels):
        c, yh, x = place(picks[t], meta)
        inner[:, t * width:(t + 1) * width] = dot(left[t], pool[(c * 2 + yh) * 4 + x]).astype(BF)
    product = dot(inner[...], right[...].reshape(channels * width, width))
    size = meta[0]
    product = jnp.where(live(size, product.shape), product, 0.0).astype(BF)
    first_out[...] = product
    message[0:width, :] = product
    value = product.astype(F32)
    columns = jnp.sum(value * value, axis=0, keepdims=True)
    squares = jnp.broadcast_to(jnp.sum(columns, axis=1, keepdims=True), (1, width))
    count = jnp.full((1, width), size * size, jnp.int32).astype(F32)
    tile = pack(squares, count)
    message[width:width + TILE, :] = tile
    stats[...] = tile
    send[half * width:half * width + TILE, :] = tile
    turned = value.T.astype(BF)
    turned_out[...] = turned
    for j in range(half):
        lv[j] = dot(left[channel(meta, 1 - meta[1], j)], product).astype(BF)
    for j in range(half):
        send[j * width:(j + 1) * width, :] = dot(turned, lv[j]).astype(BF)


def keep_kernel(meta, message, turned, left, keep, lv):
    half, width = left.shape[0] // 2, left.shape[1]
    first = message[0:width, :]
    for j in range(half):
        lv[j] = dot(left[channel(meta, meta[1], j)], first).astype(BF)
    for j in range(half):
        keep[j * width:(j + 1) * width, :] = dot(turned[...], lv[j]).astype(BF)


def core_sum_kernel(keep, stats, arrived, *outs):
    rows = keep.shape[0]
    quarter = rows // 4
    q0, c0 = unpack(stats[...])
    q1, c1 = unpack(arrived[rows:rows + TILE, :])
    tile = pack(q0 + q1, c0 + c1)
    for step, out in enumerate(outs):
        at = step * quarter
        out[0:quarter, :] = (
            keep[at:at + quarter, :].astype(F32) + arrived[at:at + quarter, :].astype(F32)
        ).astype(BF)
        out[quarter:quarter + TILE, :] = tile


def row_sum_kernel(a, b, c, d, out):
    rows = out.shape[0] - TILE
    out[0:rows, :] = (
        (a[0:rows, :].astype(F32) + b[0:rows, :].astype(F32)) + (c[0:rows, :].astype(F32) + d[0:rows, :].astype(F32))
    ).astype(BF)
    sums = [unpack(part[rows:rows + TILE, :]) for part in (a, b, c, d)]
    out[rows:rows + TILE, :] = pack(
        (sums[0][0] + sums[1][0]) + (sums[2][0] + sums[3][0]), (sums[0][1] + sums[1][1]) + (sums[2][1] + sums[3][1])
    )


def edge_kernel(factor, near, far, out):
    rows = near.shape[0] - TILE
    q0, c0 = unpack(near[rows:rows + TILE, :])
    q1, c1 = unpack(far[rows:rows + TILE, :])
    weight = factor / ((q0 + q1) / jnp.maximum(c0 + c1, 1.0) + 1e-6)
    total = near[0:rows, :].astype(F32) + far[0:rows, :].astype(F32)
    out[...] = (total * weight).astype(BF)


def pool_two_kernel(meta, picks, pool, left, right, g_out, base):
    channels, width = left.shape[0], left.shape[1]
    span = width + TILE
    squares = count = jnp.zeros((1, width), F32)
    for at in range(16):
        q, c = unpack(pool[at * span + width:(at + 1) * span, :])
        squares, count = squares + q, count + c
    scale = lax.rsqrt(squares / count + 1e-6)
    for t in range(channels):
        c, yh, x = place(picks[t], meta)
        start = pl.multiple_of(((c * 4 + x) * 2 + yh) * span, TILE)
        g_out[t] = (dot(pool[pl.ds(start, width), :], right[t]) * scale).astype(BF)
    total = dot(left[0], g_out[0])
    for t in range(1, channels):
        total = total + dot(left[t], g_out[t])
    base[...] = total


def half_kernel(final, meta, edges, g, start, out):
    width = g.shape[1]
    side = meta[1] if not final else 1 - meta[1]
    total = start[...]
    for j in range(edges.shape[0] // width):
        total = total + dot(edges[j * width:(j + 1) * width, :], g[channel(meta, side, j)])
    if final:
        total = jnp.where(live(meta[0], total.shape), total, 0.0)
    out[...] = total.astype(out.dtype)


def call(kernel, shapes, specs, scratch, flops, moved):
    several = isinstance(shapes, (list, tuple))
    return pl.pallas_call(
        kernel,
        out_shape=[jax.ShapeDtypeStruct(*s) for s in shapes] if several else shapes,
        in_specs=specs,
        out_specs=[VMEM] * len(shapes) if several else VMEM,
        scratch_shapes=scratch,
        compiler_params=PARAMS,
        cost_estimate=pl.CostEstimate(flops=flops, bytes_accessed=moved, transcendentals=0),
    )


def one(shape, dtype):
    return jax.ShapeDtypeStruct(shape, dtype)


def along_x(value, step):
    count = lax.axis_size("x")
    return lax.ppermute(value, "x", [(i, (i + step) % count) for i in range(count)])


def round_x(value):
    far = along_x(value, 2)
    return [value, along_x(value, 3), far, along_x(value, 1)]


def routes(z_count, y_count):
    def at(z, yl, yh):
        return (z * y_count + yl) * 2 + yh

    near, far = [], []
    for z in range(z_count):
        for yl in range(y_count):
            for yh in range(2):
                if yl + 1 < y_count:
                    following = (z, yl + 1, yh)
                elif z + 1 < z_count:
                    following = (z + 1, 0, 1 - yh)
                else:
                    continue
                near.append((at(z, yl, yh), at(*following)))
                far.append((at(z, yl, yh), at(following[0], following[1], 1 - following[2])))
    return near, far


def body(wave, left_block_environment, right_block_environment, source_block, sector_size):
    left = left_block_environment[0, 0]
    right = right_block_environment[0, 0]
    picks = source_block[0, 0]
    size = sector_size[0, 0]
    channels, width = left.shape[0], left.shape[1]
    half = channels // 2
    span = width + TILE
    unit = 2 * channels * width**3
    block_bytes = width * width * 2
    meta = jnp.stack([size, *(lax.axis_index(axis).astype(jnp.int32) for axis in ("c", "yh", "x"))])

    masked = jnp.where(live(size, (width, width)), wave[0, 0], jnp.zeros((), BF))
    masked_other = lax.ppermute(masked, "yh", SWAP)
    own = jnp.stack(round_x(masked))
    across = lax.ppermute(own, "c", SWAP)
    own_other = jnp.stack(round_x(masked_other))
    across_other = lax.ppermute(own_other, "c", SWAP)
    pool = jnp.concatenate([own, own_other, across, across_other], axis=0)
    stack = pltpu.VMEM((half, width, width), BF)
    first, message, stats, send, turned = call(
        first_kernel,
        [((width, width), BF), ((span, width), BF), ((TILE, width), BF),
         ((half * width + TILE, width), BF), ((width, width), BF)],
        [SMEM, SMEM, VMEM, VMEM, VMEM],
        [pltpu.VMEM((width, channels * width), BF), stack],
        3 * unit, 4 * channels * block_bytes,
    )(meta, picks, pool, left, right)

    arrived = lax.ppermute(send, "c", SWAP)
    message_other = lax.ppermute(message, "yh", SWAP)
    keep = call(
        keep_kernel, one((half * width, width), BF), [SMEM, VMEM, VMEM, VMEM], [stack], unit, 2 * channels * block_bytes
    )(meta, message, turned, left)
    parts = call(
        core_sum_kernel, [((2 * width + TILE, width), BF)] * 4, [VMEM] * 3, [], 1 << 20, 3 * half * block_bytes
    )(keep, stats, arrived)
    arrived_x = [along_x(parts[2], 2), along_x(parts[1], 1), along_x(parts[3], 3)]
    row = call(
        row_sum_kernel, one((2 * width + TILE, width), BF), [VMEM] * 4, [], 1 << 20, 10 * block_bytes
    )(parts[0], *arrived_x)
    near, far = routes(lax.axis_size("z"), lax.axis_size("yl"))
    from_far = lax.ppermute(row, YROW, far)
    from_near = lax.ppermute(row, YROW, near)

    both = jnp.concatenate([message, message_other], axis=0)
    two_own = jnp.concatenate(round_x(both))
    two_other = lax.ppermute(two_own, "c", SWAP)
    pool_two = jnp.concatenate([two_own, two_other])
    g, base = call(
        pool_two_kernel,
        [((channels, width, width), BF), ((width, width), F32)],
        [SMEM, SMEM, VMEM, VMEM, VMEM],
        [],
        2 * unit, 4 * channels * block_bytes,
    )(meta, picks, pool_two, left, right)

    factor = 1.0 / (width * math.sqrt(channels_of(sector_size)))
    edge = call(
        lambda *refs: edge_kernel(factor, *refs), one((2 * width, width), BF), [VMEM] * 2, [], 1 << 20, 12 * block_bytes
    )(from_near, from_far)
    edges_own = jnp.concatenate(round_x(edge))
    edges_other = lax.ppermute(edges_own, "c", SWAP)
    partial = call(
        lambda *refs: half_kernel(False, *refs), one((width, width), F32), [SMEM, VMEM, VMEM, VMEM], [], unit // 2,
        3 * half * block_bytes,
    )(meta, edges_own, g, base)
    second = call(
        lambda *refs: half_kernel(True, *refs), one((width, width), BF), [SMEM, VMEM, VMEM, VMEM], [], unit // 2,
        3 * half * block_bytes,
    )(meta, edges_other, g, partial)
    return (first[None, None], second[None, None])


def channels_of(sector_size):
    return sector_size.shape[1] * lax.axis_size(("x", "yh", "c"))


def solution(mesh):
    finer = Mesh(mesh.devices.reshape(mesh.shape["sec"] // 4, 4, 4, 2, 2), ("z", "yl", "x", "yh", "c"))
    sec, blk = ("z", "yl"), ("x", "yh", "c")
    return jax.shard_map(
        body,
        mesh=finer,
        in_specs=(
            P(sec, blk, None, None),
            P(sec, blk, None, None, None),
            P(sec, blk, None, None, None),
            P(sec, blk, None),
            P(sec, blk),
        ),
        out_specs=(P(sec, blk, None, None), P(sec, blk, None, None)),
        check_vma=False,
    )
```

```python
import math

import jax
import jax.numpy as jnp
from jax import lax
from jax.experimental import pallas as pl
from jax.experimental.pallas import tpu as pltpu
from jax.sharding import Mesh
from jax.sharding import PartitionSpec as P


BF = jnp.bfloat16
F32 = jnp.float32
TILE = 16
YROW = ("z", "yl", "yh")
SWAP = [(0, 1), (1, 0)]
VMEM = pl.BlockSpec(memory_space=pltpu.VMEM)
SMEM = pl.BlockSpec(memory_space=pltpu.SMEM)
ANY = pl.BlockSpec(memory_space=pl.ANY)
PARAMS = pltpu.CompilerParams(vmem_limit_bytes=16 << 20)


def dot(a, b):
    return jnp.dot(a, b, preferred_element_type=F32)


def pieces(value):
    high = value.astype(BF).astype(F32)
    mid = (value - high).astype(BF).astype(F32)
    return high, mid, value - high - mid


def pack(squares, count):
    width = squares.shape[-1]
    row = lax.broadcasted_iota(jnp.int32, (TILE, width), 0)
    tile = jnp.zeros((TILE, width), F32)
    for at, part in enumerate(pieces(squares) + pieces(count)):
        tile = jnp.where(row == at, jnp.broadcast_to(part, (TILE, width)), tile)
    return tile.astype(BF)


def unpack(tile):
    t = tile.astype(F32)
    return t[0:1] + t[1:2] + t[2:3], t[3:4] + t[4:5] + t[5:6]


def live(size, shape):
    rows = lax.broadcasted_iota(jnp.int32, shape, 0)
    columns = lax.broadcasted_iota(jnp.int32, shape, 1)
    return (rows < size) & (columns < size)


def place(source, meta):
    x, yh, c = source // 4, (source // 2) % 2, source % 2
    return lax.rem(c + meta[1], 2), lax.rem(yh + meta[2], 2), lax.rem(x + 4 - meta[3], 4)


def channel(meta, side, j):
    return side * 8 + lax.rem(meta[3] + j // 2, 4) * 2 + j % 2


def load_kernel(source, out):
    out[...] = source[...]


def first_kernel(meta, picks, own, across, left, right, first_out, message, stats, send, turned_out, pool, inner, lv):
    channels, width = left.shape[0], left.shape[1]
    half = channels // 2
    pool[0:half] = own[...]
    pool[half:channels] = across[...]
    for t in range(channels):
        c, yh, step = place(picks[t], meta)
        at = (c * 2 + yh) * 4 + step * (1 - yh) + (picks[t] // 4) * yh
        inner[:, t * width:(t + 1) * width] = dot(left[t], pool[at]).astype(BF)
    product = dot(inner[...], right[...].reshape(channels * width, width))
    size = meta[0]
    product = jnp.where(live(size, product.shape), product, 0.0).astype(BF)
    first_out[...] = product
    message[0:width, :] = product
    value = product.astype(F32)
    columns = jnp.sum(value * value, axis=0, keepdims=True)
    squares = jnp.broadcast_to(jnp.sum(columns, axis=1, keepdims=True), (1, width))
    count = jnp.full((1, width), size * size, jnp.int32).astype(F32)
    tile = pack(squares, count)
    message[width:width + TILE, :] = tile
    stats[...] = tile
    send[half * width:half * width + TILE, :] = tile
    turned = value.T.astype(BF)
    turned_out[...] = turned
    for j in range(half):
        lv[j] = dot(left[channel(meta, 1 - meta[1], j)], product).astype(BF)
    for j in range(half):
        send[j * width:(j + 1) * width, :] = dot(turned, lv[j]).astype(BF)


def keep_kernel(meta, message, turned, left, keep, lv):
    half, width = left.shape[0] // 2, left.shape[1]
    first = message[0:width, :]
    for j in range(half):
        lv[j] = dot(left[channel(meta, meta[1], j)], first).astype(BF)
    for j in range(half):
        keep[j * width:(j + 1) * width, :] = dot(turned[...], lv[j]).astype(BF)


def core_sum_kernel(keep, stats, arrived, *outs):
    rows = keep.shape[0]
    quarter = rows // 4
    q0, c0 = unpack(stats[...])
    q1, c1 = unpack(arrived[rows:rows + TILE, :])
    tile = pack(q0 + q1, c0 + c1)
    for step, out in enumerate(outs):
        at = step * quarter
        out[0:quarter, :] = (
            keep[at:at + quarter, :].astype(F32) + arrived[at:at + quarter, :].astype(F32)
        ).astype(BF)
        out[quarter:quarter + TILE, :] = tile


def row_sum_kernel(a, b, c, d, out):
    rows = out.shape[0] - TILE
    out[0:rows, :] = (
        (a[0:rows, :].astype(F32) + b[0:rows, :].astype(F32)) + (c[0:rows, :].astype(F32) + d[0:rows, :].astype(F32))
    ).astype(BF)
    sums = [unpack(part[rows:rows + TILE, :]) for part in (a, b, c, d)]
    out[rows:rows + TILE, :] = pack(
        (sums[0][0] + sums[1][0]) + (sums[2][0] + sums[3][0]), (sums[0][1] + sums[1][1]) + (sums[2][1] + sums[3][1])
    )


def edge_kernel(factor, near, far, out):
    rows = near.shape[0] - TILE
    q0, c0 = unpack(near[rows:rows + TILE, :])
    q1, c1 = unpack(far[rows:rows + TILE, :])
    weight = factor / ((q0 + q1) / jnp.maximum(c0 + c1, 1.0) + 1e-6)
    total = near[0:rows, :].astype(F32) + far[0:rows, :].astype(F32)
    out[...] = (total * weight).astype(BF)


def pool_two_kernel(meta, picks, pool, left, right, g_out, base):
    channels, width = left.shape[0], left.shape[1]
    span = width + TILE
    squares = count = jnp.zeros((1, width), F32)
    for at in range(16):
        q, c = unpack(pool[at * span + width:(at + 1) * span, :])
        squares, count = squares + q, count + c
    scale = lax.rsqrt(squares / count + 1e-6)
    for t in range(channels):
        c, yh, x = place(picks[t], meta)
        start = pl.multiple_of(((c * 4 + x) * 2 + yh) * span, TILE)
        g_out[t] = (dot(pool[pl.ds(start, width), :], right[t]) * scale).astype(BF)
    total = dot(left[0], g_out[0])
    for t in range(1, channels):
        total = total + dot(left[t], g_out[t])
    base[...] = total


def half_kernel(final, meta, edges, g, start, out):
    width = g.shape[1]
    side = meta[1] if not final else 1 - meta[1]
    total = start[...]
    for j in range(edges.shape[0] // width):
        total = total + dot(edges[j * width:(j + 1) * width, :], g[channel(meta, side, j)])
    if final:
        total = jnp.where(live(meta[0], total.shape), total, 0.0)
    out[...] = total.astype(out.dtype)


def call(kernel, shapes, specs, scratch, flops, moved):
    several = isinstance(shapes, (list, tuple))
    return pl.pallas_call(
        kernel,
        out_shape=[jax.ShapeDtypeStruct(*s) for s in shapes] if several else shapes,
        in_specs=specs,
        out_specs=[VMEM] * len(shapes) if several else VMEM,
        scratch_shapes=scratch,
        compiler_params=PARAMS,
        cost_estimate=pl.CostEstimate(flops=flops, bytes_accessed=moved, transcendentals=0),
    )


def one(shape, dtype):
    return jax.ShapeDtypeStruct(shape, dtype)


def along_x(value, step):
    count = lax.axis_size("x")
    return lax.ppermute(value, "x", [(i, (i + step) % count) for i in range(count)])


def round_x(value):
    far = along_x(value, 2)
    return [value, along_x(value, 3), far, along_x(value, 1)]


def to_everyone_on_x(value):
    count = lax.axis_size("x")
    return lax.all_to_all(jnp.broadcast_to(value[None], (count, *value.shape)), "x", 0, 0, tiled=True)


def routes(z_count, y_count):
    def at(z, yl, yh):
        return (z * y_count + yl) * 2 + yh

    near, far = [], []
    for z in range(z_count):
        for yl in range(y_count):
            for yh in range(2):
                if yl + 1 < y_count:
                    following = (z, yl + 1, yh)
                elif z + 1 < z_count:
                    following = (z + 1, 0, 1 - yh)
                else:
                    continue
                near.append((at(z, yl, yh), at(*following)))
                far.append((at(z, yl, yh), at(following[0], following[1], 1 - following[2])))
    return near, far


def body(wave, left_block_environment, right_block_environment, source_block, sector_size):
    left = left_block_environment[0, 0]
    right = right_block_environment[0, 0]
    picks = source_block[0, 0]
    size = sector_size[0, 0]
    channels, width = left.shape[0], left.shape[1]
    half = channels // 2
    span = width + TILE
    unit = 2 * channels * width**3
    block_bytes = width * width * 2

    masked = jnp.where(live(size, (width, width)), wave[0, 0], jnp.zeros((), BF))
    masked_other = lax.ppermute(masked, "yh", SWAP)
    own = jnp.stack(round_x(masked))
    meta = jnp.stack([size, *(lax.axis_index(axis).astype(jnp.int32) for axis in ("c", "yh", "x"))])
    own_other = to_everyone_on_x(masked_other)
    own = jnp.concatenate(lax.optimization_barrier((own, own_other)))
    across = lax.ppermute(own, "c", SWAP)
    right_here = call(load_kernel, one(right.shape, BF), [VMEM], [], 1 << 20, 2 * channels * block_bytes)(right)
    stack = pltpu.VMEM((half, width, width), BF)
    first, message, stats, send, turned = call(
        first_kernel,
        [((width, width), BF), ((span, width), BF), ((TILE, width), BF),
         ((half * width + TILE, width), BF), ((width, width), BF)],
        [SMEM, SMEM] + [VMEM] * 4,
        [pltpu.VMEM((channels, width, width), BF), pltpu.VMEM((width, channels * width), BF), stack],
        3 * unit, 4 * channels * block_bytes,
    )(meta, picks, own, across, left, right_here)

    arrived = lax.ppermute(send, "c", SWAP)
    message_other = lax.ppermute(message, "yh", SWAP)
    keep = call(
        keep_kernel, one((half * width, width), BF), [SMEM, VMEM, VMEM, VMEM], [stack], unit, 2 * channels * block_bytes
    )(meta, message, turned, left)
    parts = call(
        core_sum_kernel, [((2 * width + TILE, width), BF)] * 4, [VMEM] * 3, [], 1 << 20, 3 * half * block_bytes
    )(keep, stats, arrived)
    arrived_x = [along_x(parts[2], 2), along_x(parts[1], 1), along_x(parts[3], 3)]
    row = call(
        row_sum_kernel, one((2 * width + TILE, width), BF), [VMEM] * 4, [], 1 << 20, 10 * block_bytes
    )(parts[0], *arrived_x)
    near, far = routes(lax.axis_size("z"), lax.axis_size("yl"))
    from_far = lax.ppermute(row, YROW, far)
    from_near = lax.ppermute(row, YROW, near)

    both = jnp.concatenate([message, message_other], axis=0)
    two_own = jnp.concatenate(round_x(both))
    two_other = lax.ppermute(two_own, "c", SWAP)
    pool_two = jnp.concatenate([two_own, two_other])
    g, base = call(
        pool_two_kernel,
        [((channels, width, width), BF), ((width, width), F32)],
        [SMEM, SMEM, VMEM, VMEM, VMEM],
        [],
        2 * unit, 4 * channels * block_bytes,
    )(meta, picks, pool_two, left, right_here)

    factor = 1.0 / (width * math.sqrt(channels_of(sector_size)))
    edge = call(
        lambda *refs: edge_kernel(factor, *refs), one((2 * width, width), BF), [VMEM] * 2, [], 1 << 20, 12 * block_bytes
    )(from_near, from_far)
    edges_own = jnp.concatenate(round_x(edge))
    edges_other = lax.ppermute(edges_own, "c", SWAP)
    partial = call(
        lambda *refs: half_kernel(False, *refs), one((width, width), F32), [SMEM, VMEM, VMEM, VMEM], [], unit // 2,
        3 * half * block_bytes,
    )(meta, edges_own, g, base)
    second = call(
        lambda *refs: half_kernel(True, *refs), one((width, width), BF), [SMEM, VMEM, VMEM, VMEM], [], unit // 2,
        3 * half * block_bytes,
    )(meta, edges_other, g, partial)
    return (first[None, None], second[None, None])


def channels_of(sector_size):
    return sector_size.shape[1] * lax.axis_size(("x", "yh", "c"))


def solution(mesh):
    finer = Mesh(mesh.devices.reshape(mesh.shape["sec"] // 4, 4, 4, 2, 2), ("z", "yl", "x", "yh", "c"))
    sec, blk = ("z", "yl"), ("x", "yh", "c")
    return jax.shard_map(
        body,
        mesh=finer,
        in_specs=(
            P(sec, blk, None, None),
            P(sec, blk, None, None, None),
            P(sec, blk, None, None, None),
            P(sec, blk, None),
            P(sec, blk),
        ),
        out_specs=(P(sec, blk, None, None), P(sec, blk, None, None)),
        check_vma=False,
    )
```

```python
import math

import jax
import jax.numpy as jnp
from jax import lax
from jax.experimental import pallas as pl
from jax.experimental.pallas import tpu as pltpu
from jax.sharding import Mesh
from jax.sharding import PartitionSpec as P


BF = jnp.bfloat16
F32 = jnp.float32
TILE = 16
YROW = ("z", "yl", "yh")
SWAP = [(0, 1), (1, 0)]
VMEM = pl.BlockSpec(memory_space=pltpu.VMEM)
SMEM = pl.BlockSpec(memory_space=pltpu.SMEM)
ANY = pl.BlockSpec(memory_space=pl.ANY)
PARAMS = pltpu.CompilerParams(vmem_limit_bytes=16 << 20)


def dot(a, b):
    return jnp.dot(a, b, preferred_element_type=F32)


def pieces(value):
    high = value.astype(BF).astype(F32)
    mid = (value - high).astype(BF).astype(F32)
    return high, mid, value - high - mid


def pack(squares, count):
    width = squares.shape[-1]
    row = lax.broadcasted_iota(jnp.int32, (TILE, width), 0)
    tile = jnp.zeros((TILE, width), F32)
    for at, part in enumerate(pieces(squares) + pieces(count)):
        tile = jnp.where(row == at, jnp.broadcast_to(part, (TILE, width)), tile)
    return tile.astype(BF)


def unpack(tile):
    t = tile.astype(F32)
    return t[0:1] + t[1:2] + t[2:3], t[3:4] + t[4:5] + t[5:6]


def live(size, shape):
    rows = lax.broadcasted_iota(jnp.int32, shape, 0)
    columns = lax.broadcasted_iota(jnp.int32, shape, 1)
    return (rows < size) & (columns < size)


def place(source, meta):
    x, yh, c = source // 4, (source // 2) % 2, source % 2
    return lax.rem(c + meta[1], 2), lax.rem(yh + meta[2], 2), lax.rem(x + 4 - meta[3], 4)


def channel(meta, side, j):
    return side * 8 + lax.rem(meta[3] + j // 2, 4) * 2 + j % 2


def load_kernel(source, out):
    out[...] = source[...]


def first_kernel(meta, picks, own, across, left, right, first_out, message, stats, send, turned_out, pool, inner, lv):
    channels, width = left.shape[0], left.shape[1]
    half = channels // 2
    pool[0:half] = own[...]
    pool[half:channels] = across[...]
    for t in range(channels):
        c, yh, step = place(picks[t], meta)
        at = (c * 2 + yh) * 4 + step * (1 - yh) + (picks[t] // 4) * yh
        inner[:, t * width:(t + 1) * width] = dot(left[t], pool[at]).astype(BF)
    product = dot(inner[...], right[...].reshape(channels * width, width))
    size = meta[0]
    product = jnp.where(live(size, product.shape), product, 0.0).astype(BF)
    first_out[...] = product
    message[0:width, :] = product
    value = product.astype(F32)
    columns = jnp.sum(value * value, axis=0, keepdims=True)
    squares = jnp.broadcast_to(jnp.sum(columns, axis=1, keepdims=True), (1, width))
    count = jnp.full((1, width), size * size, jnp.int32).astype(F32)
    tile = pack(squares, count)
    message[width:width + TILE, :] = tile
    stats[...] = tile
    send[half * width:half * width + TILE, :] = tile
    turned = value.T.astype(BF)
    turned_out[...] = turned
    for j in range(half):
        lv[j] = dot(left[channel(meta, 1 - meta[1], j)], product).astype(BF)
    for j in range(half):
        send[j * width:(j + 1) * width, :] = dot(turned, lv[j]).astype(BF)


def keep_kernel(meta, message, turned, left, keep, lv):
    half, width = left.shape[0] // 2, left.shape[1]
    first = message[0:width, :]
    for j in range(half):
        lv[j] = dot(left[channel(meta, meta[1], j)], first).astype(BF)
    for j in range(half):
        keep[j * width:(j + 1) * width, :] = dot(turned[...], lv[j]).astype(BF)


def core_sum_kernel(keep, stats, arrived, *outs):
    rows = keep.shape[0]
    quarter = rows // 4
    q0, c0 = unpack(stats[...])
    q1, c1 = unpack(arrived[rows:rows + TILE, :])
    tile = pack(q0 + q1, c0 + c1)
    for step, out in enumerate(outs):
        at = step * quarter
        out[0:quarter, :] = (
            keep[at:at + quarter, :].astype(F32) + arrived[at:at + quarter, :].astype(F32)
        ).astype(BF)
        out[quarter:quarter + TILE, :] = tile


def row_sum_kernel(a, b, c, d, out):
    rows = out.shape[0] - TILE
    out[0:rows, :] = (
        (a[0:rows, :].astype(F32) + b[0:rows, :].astype(F32)) + (c[0:rows, :].astype(F32) + d[0:rows, :].astype(F32))
    ).astype(BF)
    sums = [unpack(part[rows:rows + TILE, :]) for part in (a, b, c, d)]
    out[rows:rows + TILE, :] = pack(
        (sums[0][0] + sums[1][0]) + (sums[2][0] + sums[3][0]), (sums[0][1] + sums[1][1]) + (sums[2][1] + sums[3][1])
    )


def edge_kernel(factor, near, far, out):
    rows = near.shape[0] - TILE
    q0, c0 = unpack(near[rows:rows + TILE, :])
    q1, c1 = unpack(far[rows:rows + TILE, :])
    weight = factor / ((q0 + q1) / jnp.maximum(c0 + c1, 1.0) + 1e-6)
    total = near[0:rows, :].astype(F32) + far[0:rows, :].astype(F32)
    out[...] = (total * weight).astype(BF)


def pool_two_kernel(meta, picks, pool, left, right, g_out, base):
    channels, width = left.shape[0], left.shape[1]
    span = width + TILE
    squares = count = jnp.zeros((1, width), F32)
    for at in range(16):
        q, c = unpack(pool[at * span + width:(at + 1) * span, :])
        squares, count = squares + q, count + c
    scale = lax.rsqrt(squares / count + 1e-6)
    for t in range(channels):
        c, yh, x = place(picks[t], meta)
        start = pl.multiple_of(((c * 4 + x) * 2 + yh) * span, TILE)
        g_out[t] = (dot(pool[pl.ds(start, width), :], right[t]) * scale).astype(BF)
    total = dot(left[0], g_out[0])
    for t in range(1, channels):
        total = total + dot(left[t], g_out[t])
    base[...] = total


def early_kernel(meta, own, other, g, start, out):
    width = g.shape[1]
    total = start[...]
    for edges, side in ((own, meta[1]), (other, 1 - meta[1])):
        for at, step in enumerate((0, 1, 3)):
            for i in range(2):
                row = (at * 2 + i) * width
                total = total + dot(edges[row:row + width, :], g[channel(meta, side, step * 2 + i)])
    out[...] = total


def late_kernel(final, meta, edges, g, start, out):
    width = g.shape[1]
    side = meta[1] if not final else 1 - meta[1]
    total = start[...]
    for i in range(2):
        total = total + dot(edges[i * width:(i + 1) * width, :], g[channel(meta, side, 4 + i)])
    if final:
        total = jnp.where(live(meta[0], total.shape), total, 0.0)
    out[...] = total.astype(out.dtype)


def call(kernel, shapes, specs, scratch, flops, moved):
    several = isinstance(shapes, (list, tuple))
    return pl.pallas_call(
        kernel,
        out_shape=[jax.ShapeDtypeStruct(*s) for s in shapes] if several else shapes,
        in_specs=specs,
        out_specs=[VMEM] * len(shapes) if several else VMEM,
        scratch_shapes=scratch,
        compiler_params=PARAMS,
        cost_estimate=pl.CostEstimate(flops=flops, bytes_accessed=moved, transcendentals=0),
    )


def one(shape, dtype):
    return jax.ShapeDtypeStruct(shape, dtype)


def along_x(value, step):
    count = lax.axis_size("x")
    return lax.ppermute(value, "x", [(i, (i + step) % count) for i in range(count)])


def round_x(value):
    far = along_x(value, 2)
    return [value, along_x(value, 3), far, along_x(value, 1)]


def to_everyone_on_x(value):
    count = lax.axis_size("x")
    return lax.all_to_all(jnp.broadcast_to(value[None], (count, *value.shape)), "x", 0, 0, tiled=True)


def routes(z_count, y_count):
    def at(z, yl, yh):
        return (z * y_count + yl) * 2 + yh

    near, far = [], []
    for z in range(z_count):
        for yl in range(y_count):
            for yh in range(2):
                if yl + 1 < y_count:
                    following = (z, yl + 1, yh)
                elif z + 1 < z_count:
                    following = (z + 1, 0, 1 - yh)
                else:
                    continue
                near.append((at(z, yl, yh), at(*following)))
                far.append((at(z, yl, yh), at(following[0], following[1], 1 - following[2])))
    return near, far


def body(wave, left_block_environment, right_block_environment, source_block, sector_size):
    left = left_block_environment[0, 0]
    right = right_block_environment[0, 0]
    picks = source_block[0, 0]
    size = sector_size[0, 0]
    channels, width = left.shape[0], left.shape[1]
    half = channels // 2
    span = width + TILE
    unit = 2 * channels * width**3
    block_bytes = width * width * 2

    masked = jnp.where(live(size, (width, width)), wave[0, 0], jnp.zeros((), BF))
    masked_other = lax.ppermute(masked, "yh", SWAP)
    own = jnp.stack(round_x(masked))
    meta = jnp.stack([size, *(lax.axis_index(axis).astype(jnp.int32) for axis in ("c", "yh", "x"))])
    own_other = to_everyone_on_x(masked_other)
    own = jnp.concatenate(lax.optimization_barrier((own, own_other)))
    across = lax.ppermute(own, "c", SWAP)
    right_here = call(load_kernel, one(right.shape, BF), [VMEM], [], 1 << 20, 2 * channels * block_bytes)(right)
    stack = pltpu.VMEM((half, width, width), BF)
    first, message, stats, send, turned = call(
        first_kernel,
        [((width, width), BF), ((span, width), BF), ((TILE, width), BF),
         ((half * width + TILE, width), BF), ((width, width), BF)],
        [SMEM, SMEM] + [VMEM] * 4,
        [pltpu.VMEM((channels, width, width), BF), pltpu.VMEM((width, channels * width), BF), stack],
        3 * unit, 4 * channels * block_bytes,
    )(meta, picks, own, across, left, right_here)

    arrived = lax.ppermute(send, "c", SWAP)
    message_other = lax.ppermute(message, "yh", SWAP)
    keep = call(
        keep_kernel, one((half * width, width), BF), [SMEM, VMEM, VMEM, VMEM], [stack], unit, 2 * channels * block_bytes
    )(meta, message, turned, left)
    parts = call(
        core_sum_kernel, [((2 * width + TILE, width), BF)] * 4, [VMEM] * 3, [], 1 << 20, 3 * half * block_bytes
    )(keep, stats, arrived)
    arrived_x = [along_x(parts[2], 2), along_x(parts[1], 1), along_x(parts[3], 3)]
    row = call(
        row_sum_kernel, one((2 * width + TILE, width), BF), [VMEM] * 4, [], 1 << 20, 10 * block_bytes
    )(parts[0], *arrived_x)
    near, far = routes(lax.axis_size("z"), lax.axis_size("yl"))
    from_far = lax.ppermute(row, YROW, far)
    from_near = lax.ppermute(row, YROW, near)

    both = jnp.concatenate([message, message_other], axis=0)
    two_own = jnp.concatenate(round_x(both))
    two_other = lax.ppermute(two_own, "c", SWAP)
    pool_two = jnp.concatenate([two_own, two_other])
    g, base = call(
        pool_two_kernel,
        [((channels, width, width), BF), ((width, width), F32)],
        [SMEM, SMEM, VMEM, VMEM, VMEM],
        [],
        2 * unit, 4 * channels * block_bytes,
    )(meta, picks, pool_two, left, right_here)

    factor = 1.0 / (width * math.sqrt(channels_of(sector_size)))
    edge = call(
        lambda *refs: edge_kernel(factor, *refs), one((2 * width, width), BF), [VMEM] * 2, [], 1 << 20, 12 * block_bytes
    )(from_near, from_far)
    edges_near = jnp.concatenate([edge, along_x(edge, 3), along_x(edge, 1)])
    edges_far = along_x(edge, 2)
    other_near = lax.ppermute(edges_near, "c", SWAP)
    other_far = lax.ppermute(edges_far, "c", SWAP)
    partial = call(early_kernel, one((width, width), F32), [SMEM] + [VMEM] * 4, [], unit, 4 * half * block_bytes)(
        meta, edges_near, other_near, g, base
    )
    partial = call(
        lambda *refs: late_kernel(False, *refs), one((width, width), F32), [SMEM] + [VMEM] * 3, [], unit // 8,
        half * block_bytes,
    )(meta, edges_far, g, partial)
    second = call(
        lambda *refs: late_kernel(True, *refs), one((width, width), BF), [SMEM] + [VMEM] * 3, [], unit // 8,
        half * block_bytes,
    )(meta, other_far, g, partial)
    return (first[None, None], second[None, None])


def channels_of(sector_size):
    return sector_size.shape[1] * lax.axis_size(("x", "yh", "c"))


def solution(mesh):
    finer = Mesh(mesh.devices.reshape(mesh.shape["sec"] // 4, 4, 4, 2, 2), ("z", "yl", "x", "yh", "c"))
    sec, blk = ("z", "yl"), ("x", "yh", "c")
    return jax.shard_map(
        body,
        mesh=finer,
        in_specs=(
            P(sec, blk, None, None),
            P(sec, blk, None, None, None),
            P(sec, blk, None, None, None),
            P(sec, blk, None),
            P(sec, blk),
        ),
        out_specs=(P(sec, blk, None, None), P(sec, blk, None, None)),
        check_vma=False,
    )
```

```python
import math

import jax
import jax.numpy as jnp
from jax import lax
from jax.experimental import pallas as pl
from jax.experimental.pallas import tpu as pltpu
from jax.sharding import Mesh
from jax.sharding import PartitionSpec as P


BF = jnp.bfloat16
F32 = jnp.float32
TILE = 8
YROW = ("z", "yl", "yh")
SWAP = [(0, 1), (1, 0)]
VMEM = pl.BlockSpec(memory_space=pltpu.VMEM)
SMEM = pl.BlockSpec(memory_space=pltpu.SMEM)
ANY = pl.BlockSpec(memory_space=pl.ANY)
PARAMS = pltpu.CompilerParams(vmem_limit_bytes=16 << 20)


def dot(a, b):
    return jnp.dot(a, b, preferred_element_type=F32)


def pieces(value):
    high = value.astype(BF).astype(F32)
    mid = (value - high).astype(BF).astype(F32)
    return high, mid, value - high - mid


def pack(squares, count):
    width = squares.shape[-1]
    row = lax.broadcasted_iota(jnp.int32, (TILE, width), 0)
    tile = jnp.zeros((TILE, width), F32)
    for at, part in enumerate(pieces(squares) + pieces(count)):
        tile = jnp.where(row == at, jnp.broadcast_to(part, (TILE, width)), tile)
    return tile.astype(BF)


def unpack(tile):
    t = tile.astype(F32)
    return t[0:1] + t[1:2] + t[2:3], t[3:4] + t[4:5] + t[5:6]


def live(size, shape):
    rows = lax.broadcasted_iota(jnp.int32, shape, 0)
    columns = lax.broadcasted_iota(jnp.int32, shape, 1)
    return (rows < size) & (columns < size)


def place(source, meta):
    x, yh, c = source // 4, (source // 2) % 2, source % 2
    return lax.rem(c + meta[1], 2), lax.rem(yh + meta[2], 2), lax.rem(x + 4 - meta[3], 4)


def channel(meta, side, j):
    return side * 8 + lax.rem(meta[3] + j // 2, 4) * 2 + j % 2


def load_kernel(source, out):
    out[...] = source[...]


def first_kernel(meta, picks, own, across, left, right, first_out, message, pool, inner):
    channels, width = left.shape[0], left.shape[1]
    half = channels // 2
    pool[0:half] = own[...]
    pool[half:channels] = across[...]
    for t in range(channels):
        c, yh, step = place(picks[t], meta)
        at = (c * 2 + yh) * 4 + step * (1 - yh) + (picks[t] // 4) * yh
        inner[:, t * width:(t + 1) * width] = dot(left[t], pool[at]).astype(BF)
    product = dot(inner[...], right[...].reshape(channels * width, width))
    size = meta[0]
    product = jnp.where(live(size, product.shape), product, 0.0).astype(BF)
    first_out[...] = product
    message[0:width, :] = product
    value = product.astype(F32)
    columns = jnp.sum(value * value, axis=0, keepdims=True)
    squares = jnp.broadcast_to(jnp.sum(columns, axis=1, keepdims=True), (1, width))
    count = jnp.full((1, width), size * size, jnp.int32).astype(F32)
    message[width:width + TILE, :] = pack(squares, count)


def terms(message, left_of, lv, count):
    width = message.shape[1]
    first = message[0:width, :]
    turned = first.astype(F32).T.astype(BF)
    for j in range(count):
        lv[j] = dot(left_of(j), first).astype(BF)
    return [lambda j=j: dot(turned, lv[j]) for j in range(count)]


def keep_kernel(meta, message, left, keep, lv):
    half = left.shape[0] // 2
    for j, term in enumerate(terms(message, lambda j: left[channel(meta, meta[1], j)], lv, half)):
        keep[j] = term()


def core_sum_kernel(meta, message, keep, left, *refs):
    own, lv, outs = refs[0], refs[-1], refs[1:-1]
    half, width = left.shape[0] // 2, left.shape[1]
    q0, c0 = unpack(own[width:width + TILE, :])
    q1, c1 = unpack(message[width:width + TILE, :])
    tile = pack(q0 + q1, c0 + c1)
    for out in outs:
        out[2 * width:2 * width + TILE, :] = tile
    for j, term in enumerate(terms(message, lambda j: left[channel(meta, meta[1], j)], lv, half)):
        outs[j // 2][(j % 2) * width:(j % 2 + 1) * width, :] = (keep[j] + term()).astype(BF)


def row_sum_kernel(a, b, c, d, out):
    rows = out.shape[0] - TILE
    out[0:rows, :] = (
        (a[0:rows, :].astype(F32) + b[0:rows, :].astype(F32)) + (c[0:rows, :].astype(F32) + d[0:rows, :].astype(F32))
    ).astype(BF)
    sums = [unpack(part[rows:rows + TILE, :]) for part in (a, b, c, d)]
    out[rows:rows + TILE, :] = pack(
        (sums[0][0] + sums[1][0]) + (sums[2][0] + sums[3][0]), (sums[0][1] + sums[1][1]) + (sums[2][1] + sums[3][1])
    )


def edge_kernel(factor, near, far, out):
    rows = near.shape[0] - TILE
    q0, c0 = unpack(near[rows:rows + TILE, :])
    q1, c1 = unpack(far[rows:rows + TILE, :])
    weight = factor / ((q0 + q1) / jnp.maximum(c0 + c1, 1.0) + 1e-6)
    total = near[0:rows, :].astype(F32) + far[0:rows, :].astype(F32)
    out[...] = (total * weight).astype(BF)


def pool_two_kernel(meta, picks, pool, left, right, g_out, base):
    channels, width = left.shape[0], left.shape[1]
    span = width + TILE
    squares = count = jnp.zeros((1, width), F32)
    for at in range(16):
        q, c = unpack(pool[at * span + width:(at + 1) * span, :])
        squares, count = squares + q, count + c
    scale = lax.rsqrt(squares / count + 1e-6)
    for t in range(channels):
        c, yh, x = place(picks[t], meta)
        start = pl.multiple_of(((c * 4 + x) * 2 + yh) * span, TILE)
        g_out[t] = (dot(pool[pl.ds(start, width), :], right[t]) * scale).astype(BF)
    total = dot(left[0], g_out[0])
    for t in range(1, channels):
        total = total + dot(left[t], g_out[t])
    base[...] = total


def half_kernel(final, meta, edges, g, start, out):
    width = g.shape[1]
    side = meta[1] if not final else 1 - meta[1]
    total = start[...]
    for j in range(edges.shape[0] // width):
        total = total + dot(edges[j * width:(j + 1) * width, :], g[channel(meta, side, j)])
    if final:
        total = jnp.where(live(meta[0], total.shape), total, 0.0)
    out[...] = total.astype(out.dtype)


def call(kernel, shapes, specs, scratch, flops, moved):
    several = isinstance(shapes, (list, tuple))
    return pl.pallas_call(
        kernel,
        out_shape=[jax.ShapeDtypeStruct(*s) for s in shapes] if several else shapes,
        in_specs=specs,
        out_specs=[VMEM] * len(shapes) if several else VMEM,
        scratch_shapes=scratch,
        compiler_params=PARAMS,
        cost_estimate=pl.CostEstimate(flops=flops, bytes_accessed=moved, transcendentals=0),
    )


def one(shape, dtype):
    return jax.ShapeDtypeStruct(shape, dtype)


def along_x(value, step):
    count = lax.axis_size("x")
    return lax.ppermute(value, "x", [(i, (i + step) % count) for i in range(count)])


def round_x(value):
    far = along_x(value, 2)
    return [value, along_x(value, 3), far, along_x(value, 1)]


def to_everyone_on_x(value):
    count = lax.axis_size("x")
    return lax.all_to_all(jnp.broadcast_to(value[None], (count, *value.shape)), "x", 0, 0, tiled=True)


def routes(z_count, y_count):
    def at(z, yl, yh):
        return (z * y_count + yl) * 2 + yh

    near, far = [], []
    for z in range(z_count):
        for yl in range(y_count):
            for yh in range(2):
                if yl + 1 < y_count:
                    following = (z, yl + 1, yh)
                elif z + 1 < z_count:
                    following = (z + 1, 0, 1 - yh)
                else:
                    continue
                near.append((at(z, yl, yh), at(*following)))
                far.append((at(z, yl, yh), at(following[0], following[1], 1 - following[2])))
    return near, far


def body(wave, left_block_environment, right_block_environment, source_block, sector_size):
    left = left_block_environment[0, 0]
    right = right_block_environment[0, 0]
    picks = source_block[0, 0]
    size = sector_size[0, 0]
    channels, width = left.shape[0], left.shape[1]
    half = channels // 2
    span = width + TILE
    unit = 2 * channels * width**3
    block_bytes = width * width * 2

    masked = jnp.where(live(size, (width, width)), wave[0, 0], jnp.zeros((), BF))
    masked_other = lax.ppermute(masked, "yh", SWAP)
    own = jnp.stack(round_x(masked))
    meta = jnp.stack([size, *(lax.axis_index(axis).astype(jnp.int32) for axis in ("c", "yh", "x"))])
    own_other = to_everyone_on_x(masked_other)
    own = jnp.concatenate(lax.optimization_barrier((own, own_other)))
    across = lax.ppermute(own, "c", SWAP)
    right_here = call(load_kernel, one(right.shape, BF), [VMEM], [], 1 << 20, 2 * channels * block_bytes)(right)
    left_other = lax.ppermute(left, "c", SWAP)
    stack = pltpu.VMEM((half, width, width), BF)
    first, message = call(
        first_kernel, [((width, width), BF), ((span, width), BF)], [SMEM, SMEM] + [VMEM] * 4,
        [pltpu.VMEM((channels, width, width), BF), pltpu.VMEM((width, channels * width), BF)],
        2 * unit, 4 * channels * block_bytes,
    )(meta, picks, own, across, left, right_here)

    message_core = lax.ppermute(message, "c", SWAP)
    message_other = lax.ppermute(message, "yh", SWAP)
    keep = call(
        keep_kernel, one((half, width, width), F32), [SMEM, VMEM, VMEM], [stack], unit, 2 * channels * block_bytes
    )(meta, message, left)
    parts = call(
        core_sum_kernel, [((2 * width + TILE, width), BF)] * 4, [SMEM] + [VMEM] * 4, [stack], unit, 3 * half * block_bytes
    )(meta, message_core, keep, left_other, message)
    arrived_x = [along_x(parts[2], 2), along_x(parts[1], 1), along_x(parts[3], 3)]
    row = call(
        row_sum_kernel, one((2 * width + TILE, width), BF), [VMEM] * 4, [], 1 << 20, 10 * block_bytes
    )(parts[0], *arrived_x)
    near, far = routes(lax.axis_size("z"), lax.axis_size("yl"))
    from_far = lax.ppermute(row, YROW, far)
    from_near = lax.ppermute(row, YROW, near)

    both = jnp.concatenate([message, message_other], axis=0)
    two_own = jnp.concatenate(round_x(both))
    two_other = lax.ppermute(two_own, "c", SWAP)
    pool_two = jnp.concatenate([two_own, two_other])
    g, base = call(
        pool_two_kernel,
        [((channels, width, width), BF), ((width, width), F32)],
        [SMEM, SMEM, VMEM, VMEM, VMEM],
        [],
        2 * unit, 4 * channels * block_bytes,
    )(meta, picks, pool_two, left, right_here)

    factor = 1.0 / (width * math.sqrt(channels_of(sector_size)))
    edge = call(
        lambda *refs: edge_kernel(factor, *refs), one((2 * width, width), BF), [VMEM] * 2, [], 1 << 20, 12 * block_bytes
    )(from_near, from_far)
    edges_own = jnp.concatenate(round_x(edge))
    edges_other = lax.ppermute(edges_own, "c", SWAP)
    partial = call(
        lambda *refs: half_kernel(False, *refs), one((width, width), F32), [SMEM, VMEM, VMEM, VMEM], [], unit // 2,
        3 * half * block_bytes,
    )(meta, edges_own, g, base)
    second = call(
        lambda *refs: half_kernel(True, *refs), one((width, width), BF), [SMEM, VMEM, VMEM, VMEM], [], unit // 2,
        3 * half * block_bytes,
    )(meta, edges_other, g, partial)
    return (first[None, None], second[None, None])


def channels_of(sector_size):
    return sector_size.shape[1] * lax.axis_size(("x", "yh", "c"))


def solution(mesh):
    finer = Mesh(mesh.devices.reshape(mesh.shape["sec"] // 4, 4, 4, 2, 2), ("z", "yl", "x", "yh", "c"))
    sec, blk = ("z", "yl"), ("x", "yh", "c")
    return jax.shard_map(
        body,
        mesh=finer,
        in_specs=(
            P(sec, blk, None, None),
            P(sec, blk, None, None, None),
            P(sec, blk, None, None, None),
            P(sec, blk, None),
            P(sec, blk),
        ),
        out_specs=(P(sec, blk, None, None), P(sec, blk, None, None)),
        check_vma=False,
    )
```

```python
import math

import jax
import jax.numpy as jnp
from jax import lax
from jax.experimental import pallas as pl
from jax.experimental.pallas import tpu as pltpu
from jax.sharding import Mesh
from jax.sharding import PartitionSpec as P


BF = jnp.bfloat16
F32 = jnp.float32
TILE = 8
YROW = ("z", "yl", "yh")
SWAP = [(0, 1), (1, 0)]
VMEM = pl.BlockSpec(memory_space=pltpu.VMEM)
SMEM = pl.BlockSpec(memory_space=pltpu.SMEM)
ANY = pl.BlockSpec(memory_space=pl.ANY)
PARAMS = pltpu.CompilerParams(vmem_limit_bytes=16 << 20)


def dot(a, b):
    return jnp.dot(a, b, preferred_element_type=F32)


def pieces(value):
    high = value.astype(BF).astype(F32)
    mid = (value - high).astype(BF).astype(F32)
    return high, mid, value - high - mid


def pack(squares, count):
    width = squares.shape[-1]
    row = lax.broadcasted_iota(jnp.int32, (TILE, width), 0)
    tile = jnp.zeros((TILE, width), F32)
    for at, part in enumerate(pieces(squares) + pieces(count)):
        tile = jnp.where(row == at, jnp.broadcast_to(part, (TILE, width)), tile)
    return tile.astype(BF)


def unpack(tile):
    t = tile.astype(F32)
    return t[0:1] + t[1:2] + t[2:3], t[3:4] + t[4:5] + t[5:6]


def live(size, shape):
    rows = lax.broadcasted_iota(jnp.int32, shape, 0)
    columns = lax.broadcasted_iota(jnp.int32, shape, 1)
    return (rows < size) & (columns < size)


def place(source, meta):
    x, yh, c = source // 4, (source // 2) % 2, source % 2
    return lax.rem(c + meta[1], 2), lax.rem(yh + meta[2], 2), lax.rem(x + 4 - meta[3], 4)


def channel(meta, side, j):
    return side * 8 + lax.rem(meta[3] + j // 2, 4) * 2 + j % 2


def load_kernel(source, out):
    out[...] = source[...]


def first_kernel(meta, picks, own, across, left, right, first_out, message, pool, inner):
    channels, width = left.shape[0], left.shape[1]
    half = channels // 2
    pool[0:half] = own[...]
    pool[half:channels] = across[...]
    for t in range(channels):
        c, yh, step = place(picks[t], meta)
        at = (c * 2 + yh) * 4 + step * (1 - yh) + (picks[t] // 4) * yh
        inner[:, t * width:(t + 1) * width] = dot(left[t], pool[at]).astype(BF)
    product = dot(inner[...], right[...].reshape(channels * width, width))
    size = meta[0]
    product = jnp.where(live(size, product.shape), product, 0.0).astype(BF)
    first_out[...] = product
    message[0:width, :] = product
    value = product.astype(F32)
    columns = jnp.sum(value * value, axis=0, keepdims=True)
    squares = jnp.broadcast_to(jnp.sum(columns, axis=1, keepdims=True), (1, width))
    count = jnp.full((1, width), size * size, jnp.int32).astype(F32)
    message[width:width + TILE, :] = pack(squares, count)


def terms(message, left_of, lv, count):
    width = message.shape[1]
    first = message[0:width, :]
    turned = first.astype(F32).T.astype(BF)
    for j in range(count):
        lv[j] = dot(left_of(j), first).astype(BF)
    return [lambda j=j: dot(turned, lv[j]) for j in range(count)]


def keep_kernel(meta, message, left, keep, lv):
    half = left.shape[0] // 2
    for j, term in enumerate(terms(message, lambda j: left[channel(meta, meta[1], j)], lv, half)):
        keep[j] = term()


def core_sum_kernel(meta, message, keep, left, *refs):
    own, lv, outs = refs[0], refs[-1], refs[1:-1]
    half, width = left.shape[0] // 2, left.shape[1]
    q0, c0 = unpack(own[width:width + TILE, :])
    q1, c1 = unpack(message[width:width + TILE, :])
    tile = pack(q0 + q1, c0 + c1)
    for out in outs:
        out[2 * width:2 * width + TILE, :] = tile
    for j, term in enumerate(terms(message, lambda j: left[channel(meta, meta[1], j)], lv, half)):
        outs[j // 2][(j % 2) * width:(j % 2 + 1) * width, :] = (keep[j] + term()).astype(BF)


def row_sum_kernel(a, b, c, d, out):
    rows = out.shape[0] - TILE
    out[0:rows, :] = (
        (a[0:rows, :].astype(F32) + b[0:rows, :].astype(F32)) + (c[0:rows, :].astype(F32) + d[0:rows, :].astype(F32))
    ).astype(BF)
    sums = [unpack(part[rows:rows + TILE, :]) for part in (a, b, c, d)]
    out[rows:rows + TILE, :] = pack(
        (sums[0][0] + sums[1][0]) + (sums[2][0] + sums[3][0]), (sums[0][1] + sums[1][1]) + (sums[2][1] + sums[3][1])
    )


def edge_kernel(factor, near, far, out):
    rows = near.shape[0] - TILE
    q0, c0 = unpack(near[rows:rows + TILE, :])
    q1, c1 = unpack(far[rows:rows + TILE, :])
    weight = factor / ((q0 + q1) / jnp.maximum(c0 + c1, 1.0) + 1e-6)
    total = near[0:rows, :].astype(F32) + far[0:rows, :].astype(F32)
    out[...] = (total * weight).astype(BF)


def pool_two_kernel(meta, picks, pool, left, right, g_own, g_send, base, g):
    channels, width = left.shape[0], left.shape[1]
    half = channels // 2
    span = width + TILE
    squares = count = jnp.zeros((1, width), F32)
    for at in range(16):
        q, c = unpack(pool[at * span + width:(at + 1) * span, :])
        squares, count = squares + q, count + c
    scale = lax.rsqrt(squares / count + 1e-6)
    for j in range(channels):
        t = channel(meta, lax.rem(meta[1] + j // half, 2), j % half)
        c, yh, step = place(picks[t], meta)
        start = pl.multiple_of(((c * 4 + step) * 2 + yh) * span, TILE)
        block = (dot(pool[pl.ds(start, width), :], right[t]) * scale).astype(BF)
        (g_own if j < half else g_send)[j % half] = block
        g[j] = left[t]
    total = dot(g[0], g_own[0])
    for j in range(1, half):
        total = total + dot(g[j], g_own[j])
    for j in range(half):
        total = total + dot(g[half + j], g_send[j])
    base[...] = total


def other_kernel(edges, g, out):
    width = g.shape[1]
    total = dot(edges[0:width, :], g[0])
    for j in range(1, g.shape[0]):
        total = total + dot(edges[j * width:(j + 1) * width, :], g[j])
    out[...] = total


def own_kernel(edges, g, base, out):
    width = g.shape[1]
    total = base[...]
    for j in range(g.shape[0]):
        total = total + dot(edges[j * width:(j + 1) * width, :], g[j])
    out[...] = total


def second_kernel(meta, own, other, out):
    total = own[...] + other[...]
    out[...] = jnp.where(live(meta[0], total.shape), total, 0.0).astype(out.dtype)


def call(kernel, shapes, specs, scratch, flops, moved):
    several = isinstance(shapes, (list, tuple))
    return pl.pallas_call(
        kernel,
        out_shape=[jax.ShapeDtypeStruct(*s) for s in shapes] if several else shapes,
        in_specs=specs,
        out_specs=[VMEM] * len(shapes) if several else VMEM,
        scratch_shapes=scratch,
        compiler_params=PARAMS,
        cost_estimate=pl.CostEstimate(flops=flops, bytes_accessed=moved, transcendentals=0),
    )


def one(shape, dtype):
    return jax.ShapeDtypeStruct(shape, dtype)


def along_x(value, step):
    count = lax.axis_size("x")
    return lax.ppermute(value, "x", [(i, (i + step) % count) for i in range(count)])


def round_x(value):
    far = along_x(value, 2)
    return [value, along_x(value, 3), far, along_x(value, 1)]


def to_everyone_on_x(value):
    count = lax.axis_size("x")
    return lax.all_to_all(jnp.broadcast_to(value[None], (count, *value.shape)), "x", 0, 0, tiled=True)


def routes(z_count, y_count):
    def at(z, yl, yh):
        return (z * y_count + yl) * 2 + yh

    near, far = [], []
    for z in range(z_count):
        for yl in range(y_count):
            for yh in range(2):
                if yl + 1 < y_count:
                    following = (z, yl + 1, yh)
                elif z + 1 < z_count:
                    following = (z + 1, 0, 1 - yh)
                else:
                    continue
                near.append((at(z, yl, yh), at(*following)))
                far.append((at(z, yl, yh), at(following[0], following[1], 1 - following[2])))
    return near, far


def body(wave, left_block_environment, right_block_environment, source_block, sector_size):
    left = left_block_environment[0, 0]
    right = right_block_environment[0, 0]
    picks = source_block[0, 0]
    size = sector_size[0, 0]
    channels, width = left.shape[0], left.shape[1]
    half = channels // 2
    span = width + TILE
    unit = 2 * channels * width**3
    block_bytes = width * width * 2

    masked = jnp.where(live(size, (width, width)), wave[0, 0], jnp.zeros((), BF))
    masked_other = lax.ppermute(masked, "yh", SWAP)
    own = jnp.stack(round_x(masked))
    meta = jnp.stack([size, *(lax.axis_index(axis).astype(jnp.int32) for axis in ("c", "yh", "x"))])
    own_other = to_everyone_on_x(masked_other)
    own = jnp.concatenate(lax.optimization_barrier((own, own_other)))
    across = lax.ppermute(own, "c", SWAP)
    right_here = call(load_kernel, one(right.shape, BF), [VMEM], [], 1 << 20, 2 * channels * block_bytes)(right)
    left_other = lax.ppermute(left, "c", SWAP)
    stack = pltpu.VMEM((half, width, width), BF)
    first, message = call(
        first_kernel, [((width, width), BF), ((span, width), BF)], [SMEM, SMEM] + [VMEM] * 4,
        [pltpu.VMEM((channels, width, width), BF), pltpu.VMEM((width, channels * width), BF)],
        2 * unit, 4 * channels * block_bytes,
    )(meta, picks, own, across, left, right_here)

    message_core = lax.ppermute(message, "c", SWAP)
    message_other = lax.ppermute(message, "yh", SWAP)
    keep = call(
        keep_kernel, one((half, width, width), F32), [SMEM, VMEM, VMEM], [stack], unit, 2 * channels * block_bytes
    )(meta, message, left)
    parts = call(
        core_sum_kernel, [((2 * width + TILE, width), BF)] * 4, [SMEM] + [VMEM] * 4, [stack], unit, 3 * half * block_bytes
    )(meta, message_core, keep, left_other, message)
    arrived_x = [along_x(parts[2], 2), along_x(parts[1], 1), along_x(parts[3], 3)]
    row = call(
        row_sum_kernel, one((2 * width + TILE, width), BF), [VMEM] * 4, [], 1 << 20, 10 * block_bytes
    )(parts[0], *arrived_x)
    near, far = routes(lax.axis_size("z"), lax.axis_size("yl"))
    from_far = lax.ppermute(row, YROW, far)
    from_near = lax.ppermute(row, YROW, near)

    both = jnp.concatenate([message, message_other], axis=0)
    two_own = jnp.concatenate(round_x(both))
    two_other = lax.ppermute(two_own, "c", SWAP)
    pool_two = jnp.concatenate([two_own, two_other])
    g_own, g_send, base = call(
        pool_two_kernel,
        [((half, width, width), BF), ((half, width, width), BF), ((width, width), F32)],
        [SMEM, SMEM, VMEM, VMEM, VMEM],
        [pltpu.VMEM((channels, width, width), BF)],
        2 * unit, 4 * channels * block_bytes,
    )(meta, picks, pool_two, left, right_here)
    g_other = lax.ppermute(g_send, "c", SWAP)

    factor = 1.0 / (width * math.sqrt(channels_of(sector_size)))
    edge = call(
        lambda *refs: edge_kernel(factor, *refs), one((2 * width, width), BF), [VMEM] * 2, [], 1 << 20, 12 * block_bytes
    )(from_near, from_far)
    edges_own = jnp.concatenate(round_x(edge))
    for_other = call(other_kernel, one((width, width), F32), [VMEM] * 2, [], unit // 2, 3 * half * block_bytes)(
        edges_own, g_other
    )
    from_other = lax.ppermute(for_other, "c", SWAP)
    from_own = call(own_kernel, one((width, width), F32), [VMEM] * 3, [], unit // 2, 3 * half * block_bytes)(
        edges_own, g_own, base
    )
    second = call(second_kernel, one((width, width), BF), [SMEM, VMEM, VMEM], [], 1 << 18, 3 * block_bytes)(
        meta, from_own, from_other
    )
    return (first[None, None], second[None, None])


def channels_of(sector_size):
    return sector_size.shape[1] * lax.axis_size(("x", "yh", "c"))


def solution(mesh):
    finer = Mesh(mesh.devices.reshape(mesh.shape["sec"] // 4, 4, 4, 2, 2), ("z", "yl", "x", "yh", "c"))
    sec, blk = ("z", "yl"), ("x", "yh", "c")
    return jax.shard_map(
        body,
        mesh=finer,
        in_specs=(
            P(sec, blk, None, None),
            P(sec, blk, None, None, None),
            P(sec, blk, None, None, None),
            P(sec, blk, None),
            P(sec, blk),
        ),
        out_specs=(P(sec, blk, None, None), P(sec, blk, None, None)),
        check_vma=False,
    )
```

```python
import math

import jax
import jax.numpy as jnp
from jax import lax
from jax.experimental import pallas as pl
from jax.experimental.pallas import tpu as pltpu
from jax.sharding import Mesh
from jax.sharding import PartitionSpec as P


BF = jnp.bfloat16
F32 = jnp.float32
TILE = 8
YROW = ("z", "yl", "yh")
SWAP = [(0, 1), (1, 0)]
VMEM = pl.BlockSpec(memory_space=pltpu.VMEM)
SMEM = pl.BlockSpec(memory_space=pltpu.SMEM)
ANY = pl.BlockSpec(memory_space=pl.ANY)
PARAMS = pltpu.CompilerParams(vmem_limit_bytes=16 << 20)


def dot(a, b):
    return jnp.dot(a, b, preferred_element_type=F32)


def pieces(value):
    high = value.astype(BF).astype(F32)
    mid = (value - high).astype(BF).astype(F32)
    return high, mid, value - high - mid


def pack(squares, count):
    width = squares.shape[-1]
    row = lax.broadcasted_iota(jnp.int32, (TILE, width), 0)
    tile = jnp.zeros((TILE, width), F32)
    for at, part in enumerate(pieces(squares) + pieces(count)):
        tile = jnp.where(row == at, jnp.broadcast_to(part, (TILE, width)), tile)
    return tile.astype(BF)


def unpack(tile):
    t = tile.astype(F32)
    return t[0:1] + t[1:2] + t[2:3], t[3:4] + t[4:5] + t[5:6]


def live(size, shape):
    rows = lax.broadcasted_iota(jnp.int32, shape, 0)
    columns = lax.broadcasted_iota(jnp.int32, shape, 1)
    return (rows < size) & (columns < size)


def place(source, meta):
    x, yh, c = source // 4, (source // 2) % 2, source % 2
    return lax.rem(c + meta[1], 2), lax.rem(yh + meta[2], 2), lax.rem(x + 4 - meta[3], 4)


def channel(meta, side, j):
    return side * 8 + lax.rem(meta[3] + j // 2, 4) * 2 + j % 2


def load_kernel(source, out):
    out[...] = source[...]


def first_kernel(meta, picks, own, across, left, right, first_out, message, pool, inner):
    channels, width = left.shape[0], left.shape[1]
    half = channels // 2
    pool[0:half] = own[...]
    pool[half:channels] = across[...]
    for t in range(channels):
        c, yh, step = place(picks[t], meta)
        at = (c * 2 + yh) * 4 + step * (1 - yh) + (picks[t] // 4) * yh
        inner[:, t * width:(t + 1) * width] = dot(left[t], pool[at]).astype(BF)
    product = dot(inner[...], right[...].reshape(channels * width, width))
    size = meta[0]
    product = jnp.where(live(size, product.shape), product, 0.0).astype(BF)
    first_out[...] = product
    message[0:width, :] = product
    value = product.astype(F32)
    columns = jnp.sum(value * value, axis=0, keepdims=True)
    squares = jnp.broadcast_to(jnp.sum(columns, axis=1, keepdims=True), (1, width))
    count = jnp.full((1, width), size * size, jnp.int32).astype(F32)
    message[width:width + TILE, :] = pack(squares, count)


def terms(message, left_of, lv, count):
    width = message.shape[1]
    first = message[0:width, :]
    turned = first.astype(F32).T.astype(BF)
    for j in range(count):
        lv[j] = dot(left_of(j), first).astype(BF)
    return [lambda j=j: dot(turned, lv[j]) for j in range(count)]


def keep_kernel(meta, message, left, keep, lv):
    half = left.shape[0] // 2
    for j, term in enumerate(terms(message, lambda j: left[channel(meta, meta[1], j)], lv, half)):
        keep[j] = term()


def core_sum_kernel(meta, message, keep, left, *refs):
    own, lv, outs = refs[0], refs[-1], refs[1:-1]
    half, width = left.shape[0] // 2, left.shape[1]
    q0, c0 = unpack(own[width:width + TILE, :])
    q1, c1 = unpack(message[width:width + TILE, :])
    tile = pack(q0 + q1, c0 + c1)
    for out in outs:
        out[2 * width:2 * width + TILE, :] = tile
    for j, term in enumerate(terms(message, lambda j: left[channel(meta, meta[1], j)], lv, half)):
        outs[j // 2][(j % 2) * width:(j % 2 + 1) * width, :] = (keep[j] + term()).astype(BF)


def row_sum_kernel(a, b, c, d, out):
    rows = out.shape[0] - TILE
    out[0:rows, :] = (
        (a[0:rows, :].astype(F32) + b[0:rows, :].astype(F32)) + (c[0:rows, :].astype(F32) + d[0:rows, :].astype(F32))
    ).astype(BF)
    sums = [unpack(part[rows:rows + TILE, :]) for part in (a, b, c, d)]
    out[rows:rows + TILE, :] = pack(
        (sums[0][0] + sums[1][0]) + (sums[2][0] + sums[3][0]), (sums[0][1] + sums[1][1]) + (sums[2][1] + sums[3][1])
    )


def edge_kernel(factor, near, far, out):
    rows = near.shape[0] - TILE
    q0, c0 = unpack(near[rows:rows + TILE, :])
    q1, c1 = unpack(far[rows:rows + TILE, :])
    weight = factor / ((q0 + q1) / jnp.maximum(c0 + c1, 1.0) + 1e-6)
    total = near[0:rows, :].astype(F32) + far[0:rows, :].astype(F32)
    out[...] = (total * weight).astype(BF)


def vector_terms(meta, picks, pool, right, side, g_out):
    half, width = g_out.shape[0], g_out.shape[1]
    span = width + TILE
    squares = count = jnp.zeros((1, width), F32)
    for at in range(16):
        q, c = unpack(pool[at * span + width:(at + 1) * span, :])
        squares, count = squares + q, count + c
    scale = lax.rsqrt(squares / count + 1e-6)
    for j in range(half):
        t = channel(meta, side, j)
        c, yh, step = place(picks[t], meta)
        start = pl.multiple_of(((c * 4 + step) * 2 + yh) * span, TILE)
        g_out[j] = (dot(pool[pl.ds(start, width), :], right[t]) * scale).astype(BF)


def send_kernel(meta, picks, pool, right, g_send):
    vector_terms(meta, picks, pool, right, 1 - meta[1], g_send)


def pool_two_kernel(meta, picks, pool, left, right, g_send, g_own, base):
    half = g_own.shape[0]
    vector_terms(meta, picks, pool, right, meta[1], g_own)
    total = dot(left[channel(meta, meta[1], 0)], g_own[0])
    for j in range(1, half):
        total = total + dot(left[channel(meta, meta[1], j)], g_own[j])
    for j in range(half):
        total = total + dot(left[channel(meta, 1 - meta[1], j)], g_send[j])
    base[...] = total


def other_kernel(edges, g, out):
    width = g.shape[1]
    total = dot(edges[0:width, :], g[0])
    for j in range(1, g.shape[0]):
        total = total + dot(edges[j * width:(j + 1) * width, :], g[j])
    out[...] = total


def own_kernel(edges, g, base, out):
    width = g.shape[1]
    total = base[...]
    for j in range(g.shape[0]):
        total = total + dot(edges[j * width:(j + 1) * width, :], g[j])
    out[...] = total


def second_kernel(meta, own, other, out):
    total = own[...] + other[...]
    out[...] = jnp.where(live(meta[0], total.shape), total, 0.0).astype(out.dtype)


def call(kernel, shapes, specs, scratch, flops, moved):
    several = isinstance(shapes, (list, tuple))
    return pl.pallas_call(
        kernel,
        out_shape=[jax.ShapeDtypeStruct(*s) for s in shapes] if several else shapes,
        in_specs=specs,
        out_specs=[VMEM] * len(shapes) if several else VMEM,
        scratch_shapes=scratch,
        compiler_params=PARAMS,
        cost_estimate=pl.CostEstimate(flops=flops, bytes_accessed=moved, transcendentals=0),
    )


def one(shape, dtype):
    return jax.ShapeDtypeStruct(shape, dtype)


def along_x(value, step):
    count = lax.axis_size("x")
    return lax.ppermute(value, "x", [(i, (i + step) % count) for i in range(count)])


def round_x(value):
    far = along_x(value, 2)
    return [value, along_x(value, 3), far, along_x(value, 1)]


def to_everyone_on_x(value):
    count = lax.axis_size("x")
    return lax.all_to_all(jnp.broadcast_to(value[None], (count, *value.shape)), "x", 0, 0, tiled=True)


def routes(z_count, y_count):
    def at(z, yl, yh):
        return (z * y_count + yl) * 2 + yh

    near, far = [], []
    for z in range(z_count):
        for yl in range(y_count):
            for yh in range(2):
                if yl + 1 < y_count:
                    following = (z, yl + 1, yh)
                elif z + 1 < z_count:
                    following = (z + 1, 0, 1 - yh)
                else:
                    continue
                near.append((at(z, yl, yh), at(*following)))
                far.append((at(z, yl, yh), at(following[0], following[1], 1 - following[2])))
    return near, far


def body(wave, left_block_environment, right_block_environment, source_block, sector_size):
    left = left_block_environment[0, 0]
    right = right_block_environment[0, 0]
    picks = source_block[0, 0]
    size = sector_size[0, 0]
    channels, width = left.shape[0], left.shape[1]
    half = channels // 2
    span = width + TILE
    unit = 2 * channels * width**3
    block_bytes = width * width * 2

    masked = jnp.where(live(size, (width, width)), wave[0, 0], jnp.zeros((), BF))
    masked_other = lax.ppermute(masked, "yh", SWAP)
    own = jnp.stack(round_x(masked))
    meta = jnp.stack([size, *(lax.axis_index(axis).astype(jnp.int32) for axis in ("c", "yh", "x"))])
    own_other = to_everyone_on_x(masked_other)
    own = jnp.concatenate(lax.optimization_barrier((own, own_other)))
    across = lax.ppermute(own, "c", SWAP)
    right_here = call(load_kernel, one(right.shape, BF), [VMEM], [], 1 << 20, 2 * channels * block_bytes)(right)
    left_other = lax.ppermute(left, "c", SWAP)
    stack = pltpu.VMEM((half, width, width), BF)
    first, message = call(
        first_kernel, [((width, width), BF), ((span, width), BF)], [SMEM, SMEM] + [VMEM] * 4,
        [pltpu.VMEM((channels, width, width), BF), pltpu.VMEM((width, channels * width), BF)],
        2 * unit, 4 * channels * block_bytes,
    )(meta, picks, own, across, left, right_here)

    message_core = lax.ppermute(message, "c", SWAP)
    message_other = lax.ppermute(message, "yh", SWAP)
    keep = call(
        keep_kernel, one((half, width, width), F32), [SMEM, VMEM, VMEM], [stack], unit, 2 * channels * block_bytes
    )(meta, message, left)
    parts = call(
        core_sum_kernel, [((2 * width + TILE, width), BF)] * 4, [SMEM] + [VMEM] * 4, [stack], unit, 3 * half * block_bytes
    )(meta, message_core, keep, left_other, message)
    arrived_x = [along_x(parts[2], 2), along_x(parts[1], 1), along_x(parts[3], 3)]
    row = call(
        row_sum_kernel, one((2 * width + TILE, width), BF), [VMEM] * 4, [], 1 << 20, 10 * block_bytes
    )(parts[0], *arrived_x)
    near, far = routes(lax.axis_size("z"), lax.axis_size("yl"))
    from_far = lax.ppermute(row, YROW, far)
    from_near = lax.ppermute(row, YROW, near)

    both = jnp.concatenate([message, message_other], axis=0)
    two_own = jnp.concatenate(round_x(both))
    two_other = lax.ppermute(two_own, "c", SWAP)
    pool_two = jnp.concatenate([two_own, two_other])
    g_send = call(
        send_kernel, one((half, width, width), BF), [SMEM, SMEM, VMEM, VMEM], [], unit // 2, channels * block_bytes
    )(meta, picks, pool_two, right_here)
    g_other = lax.ppermute(g_send, "c", SWAP)
    g_own, base = call(
        pool_two_kernel, [((half, width, width), BF), ((width, width), F32)], [SMEM, SMEM] + [VMEM] * 4, [],
        3 * unit // 2, 4 * channels * block_bytes,
    )(meta, picks, pool_two, left, right_here, g_send)

    factor = 1.0 / (width * math.sqrt(channels_of(sector_size)))
    edge = call(
        lambda *refs: edge_kernel(factor, *refs), one((2 * width, width), BF), [VMEM] * 2, [], 1 << 20, 12 * block_bytes
    )(from_near, from_far)
    edges_own = jnp.concatenate(round_x(edge))
    for_other = call(other_kernel, one((width, width), F32), [VMEM] * 2, [], unit // 2, 3 * half * block_bytes)(
        edges_own, g_other
    )
    from_other = lax.ppermute(for_other, "c", SWAP)
    from_own = call(own_kernel, one((width, width), F32), [VMEM] * 3, [], unit // 2, 3 * half * block_bytes)(
        edges_own, g_own, base
    )
    second = call(second_kernel, one((width, width), BF), [SMEM, VMEM, VMEM], [], 1 << 18, 3 * block_bytes)(
        meta, from_own, from_other
    )
    return (first[None, None], second[None, None])


def channels_of(sector_size):
    return sector_size.shape[1] * lax.axis_size(("x", "yh", "c"))


def solution(mesh):
    finer = Mesh(mesh.devices.reshape(mesh.shape["sec"] // 4, 4, 4, 2, 2), ("z", "yl", "x", "yh", "c"))
    sec, blk = ("z", "yl"), ("x", "yh", "c")
    return jax.shard_map(
        body,
        mesh=finer,
        in_specs=(
            P(sec, blk, None, None),
            P(sec, blk, None, None, None),
            P(sec, blk, None, None, None),
            P(sec, blk, None),
            P(sec, blk),
        ),
        out_specs=(P(sec, blk, None, None), P(sec, blk, None, None)),
        check_vma=False,
    )
```

```python
import math

import jax
import jax.numpy as jnp
from jax import lax
from jax.experimental import pallas as pl
from jax.experimental.pallas import tpu as pltpu
from jax.sharding import Mesh
from jax.sharding import PartitionSpec as P


BF = jnp.bfloat16
F32 = jnp.float32
TILE = 8
YROW = ("z", "yl", "yh")
SWAP = [(0, 1), (1, 0)]
VMEM = pl.BlockSpec(memory_space=pltpu.VMEM)
SMEM = pl.BlockSpec(memory_space=pltpu.SMEM)
ANY = pl.BlockSpec(memory_space=pl.ANY)
PARAMS = pltpu.CompilerParams(vmem_limit_bytes=16 << 20)


def dot(a, b):
    return jnp.dot(a, b, preferred_element_type=F32)


def pieces(value):
    high = value.astype(BF).astype(F32)
    mid = (value - high).astype(BF).astype(F32)
    return high, mid, value - high - mid


def pack(squares, count):
    width = squares.shape[-1]
    row = lax.broadcasted_iota(jnp.int32, (TILE, width), 0)
    tile = jnp.zeros((TILE, width), F32)
    for at, part in enumerate(pieces(squares) + pieces(count)):
        tile = jnp.where(row == at, jnp.broadcast_to(part, (TILE, width)), tile)
    return tile.astype(BF)


def unpack(tile):
    t = tile.astype(F32)
    return t[0:1] + t[1:2] + t[2:3], t[3:4] + t[4:5] + t[5:6]


def live(size, shape):
    rows = lax.broadcasted_iota(jnp.int32, shape, 0)
    columns = lax.broadcasted_iota(jnp.int32, shape, 1)
    return (rows < size) & (columns < size)


def place(source, meta):
    x, yh, c = source // 4, (source // 2) % 2, source % 2
    return lax.rem(c + meta[1], 2), lax.rem(yh + meta[2], 2), lax.rem(x + 4 - meta[3], 4)


def channel(meta, side, j):
    return side * 8 + lax.rem(meta[3] + j // 2, 4) * 2 + j % 2


def load_kernel(source, out):
    out[...] = source[...]


def first_kernel(meta, picks, own, across, left, right, first_out, message, pool, inner):
    channels, width = left.shape[0], left.shape[1]
    half = channels // 2
    pool[0:half] = own[...]
    pool[half:channels] = across[...]
    for t in range(channels):
        c, yh, step = place(picks[t], meta)
        at = (c * 2 + yh) * 4 + step * (1 - yh) + (picks[t] // 4) * yh
        inner[:, t * width:(t + 1) * width] = dot(left[t], pool[at]).astype(BF)
    product = dot(inner[...], right[...].reshape(channels * width, width))
    size = meta[0]
    product = jnp.where(live(size, product.shape), product, 0.0).astype(BF)
    first_out[...] = product
    message[0:width, :] = product
    value = product.astype(F32)
    columns = jnp.sum(value * value, axis=0, keepdims=True)
    squares = jnp.broadcast_to(jnp.sum(columns, axis=1, keepdims=True), (1, width))
    count = jnp.full((1, width), size * size, jnp.int32).astype(F32)
    message[width:width + TILE, :] = pack(squares, count)


def terms(message, left_of, lv, count):
    width = message.shape[1]
    first = message[0:width, :]
    turned = first.astype(F32).T.astype(BF)
    for j in range(count):
        lv[j] = dot(left_of(j), first).astype(BF)
    return [lambda j=j: dot(turned, lv[j]) for j in range(count)]


def keep_kernel(meta, message, left, keep, lv):
    half = left.shape[0] // 2
    for j, term in enumerate(terms(message, lambda j: left[channel(meta, meta[1], j)], lv, half)):
        keep[j] = term()


def core_sum_kernel(meta, message, keep, left, *refs):
    own, lv, outs = refs[0], refs[-1], refs[1:-1]
    half, width = left.shape[0] // 2, left.shape[1]
    q0, c0 = unpack(own[width:width + TILE, :])
    q1, c1 = unpack(message[width:width + TILE, :])
    tile = pack(q0 + q1, c0 + c1)
    for out in outs:
        out[2 * width:2 * width + TILE, :] = tile
    for j, term in enumerate(terms(message, lambda j: left[channel(meta, meta[1], j)], lv, half)):
        outs[j // 2][(j % 2) * width:(j % 2 + 1) * width, :] = (keep[j] + term()).astype(BF)


def row_sum_kernel(a, b, c, d, out):
    rows = out.shape[0] - TILE
    out[0:rows, :] = (
        (a[0:rows, :].astype(F32) + b[0:rows, :].astype(F32)) + (c[0:rows, :].astype(F32) + d[0:rows, :].astype(F32))
    ).astype(BF)
    sums = [unpack(part[rows:rows + TILE, :]) for part in (a, b, c, d)]
    out[rows:rows + TILE, :] = pack(
        (sums[0][0] + sums[1][0]) + (sums[2][0] + sums[3][0]), (sums[0][1] + sums[1][1]) + (sums[2][1] + sums[3][1])
    )


def edge_kernel(factor, near, far, out):
    rows = near.shape[0] - TILE
    q0, c0 = unpack(near[rows:rows + TILE, :])
    q1, c1 = unpack(far[rows:rows + TILE, :])
    weight = factor / ((q0 + q1) / jnp.maximum(c0 + c1, 1.0) + 1e-6)
    total = near[0:rows, :].astype(F32) + far[0:rows, :].astype(F32)
    out[...] = (total * weight).astype(BF)


def vector_terms(meta, picks, pool, right, side, g_out):
    half, width = g_out.shape[0], g_out.shape[1]
    span = width + TILE
    squares = count = jnp.zeros((1, width), F32)
    for at in range(16):
        q, c = unpack(pool[at * span + width:(at + 1) * span, :])
        squares, count = squares + q, count + c
    scale = lax.rsqrt(squares / count + 1e-6)
    for j in range(half):
        t = channel(meta, side, j)
        c, yh, step = place(picks[t], meta)
        start = pl.multiple_of(((c * 4 + step) * 2 + yh) * span, TILE)
        g_out[j] = (dot(pool[pl.ds(start, width), :], right[t]) * scale).astype(BF)


def send_kernel(meta, picks, pool, right, g_send):
    vector_terms(meta, picks, pool, right, 1 - meta[1], g_send)


def pool_two_kernel(meta, picks, pool, left, right, g_send, g_own, base):
    vector_terms(meta, picks, pool, right, meta[1], g_own)
    total = dot(left[channel(meta, 1 - meta[1], 0)], g_send[0])
    for j in range(1, g_send.shape[0]):
        total = total + dot(left[channel(meta, 1 - meta[1], j)], g_send[j])
    base[...] = total


def other_kernel(edges, g, out):
    width = g.shape[1]
    total = dot(edges[0:width, :], g[0])
    for j in range(1, g.shape[0]):
        total = total + dot(edges[j * width:(j + 1) * width, :], g[j])
    out[...] = total


def own_kernel(meta, edges, left, g, base, out):
    width = g.shape[1]
    total = base[...]
    for j in range(g.shape[0]):
        updated = left[channel(meta, meta[1], j)].astype(F32) + edges[j * width:(j + 1) * width, :].astype(F32)
        total = total + dot(updated.astype(BF), g[j])
    out[...] = total


def second_kernel(meta, own, other, out):
    total = own[...] + other[...]
    out[...] = jnp.where(live(meta[0], total.shape), total, 0.0).astype(out.dtype)


def call(kernel, shapes, specs, scratch, flops, moved):
    several = isinstance(shapes, (list, tuple))
    return pl.pallas_call(
        kernel,
        out_shape=[jax.ShapeDtypeStruct(*s) for s in shapes] if several else shapes,
        in_specs=specs,
        out_specs=[VMEM] * len(shapes) if several else VMEM,
        scratch_shapes=scratch,
        compiler_params=PARAMS,
        cost_estimate=pl.CostEstimate(flops=flops, bytes_accessed=moved, transcendentals=0),
    )


def one(shape, dtype):
    return jax.ShapeDtypeStruct(shape, dtype)


def along_x(value, step):
    count = lax.axis_size("x")
    return lax.ppermute(value, "x", [(i, (i + step) % count) for i in range(count)])


def round_x(value):
    far = along_x(value, 2)
    return [value, along_x(value, 3), far, along_x(value, 1)]


def to_everyone_on_x(value):
    count = lax.axis_size("x")
    return lax.all_to_all(jnp.broadcast_to(value[None], (count, *value.shape)), "x", 0, 0, tiled=True)


def routes(z_count, y_count):
    def at(z, yl, yh):
        return (z * y_count + yl) * 2 + yh

    near, far = [], []
    for z in range(z_count):
        for yl in range(y_count):
            for yh in range(2):
                if yl + 1 < y_count:
                    following = (z, yl + 1, yh)
                elif z + 1 < z_count:
                    following = (z + 1, 0, 1 - yh)
                else:
                    continue
                near.append((at(z, yl, yh), at(*following)))
                far.append((at(z, yl, yh), at(following[0], following[1], 1 - following[2])))
    return near, far


def body(wave, left_block_environment, right_block_environment, source_block, sector_size):
    left = left_block_environment[0, 0]
    right = right_block_environment[0, 0]
    picks = source_block[0, 0]
    size = sector_size[0, 0]
    channels, width = left.shape[0], left.shape[1]
    half = channels // 2
    span = width + TILE
    unit = 2 * channels * width**3
    block_bytes = width * width * 2

    masked = jnp.where(live(size, (width, width)), wave[0, 0], jnp.zeros((), BF))
    masked_other = lax.ppermute(masked, "yh", SWAP)
    own = jnp.stack(round_x(masked))
    meta = jnp.stack([size, *(lax.axis_index(axis).astype(jnp.int32) for axis in ("c", "yh", "x"))])
    own_other = to_everyone_on_x(masked_other)
    own = jnp.concatenate(lax.optimization_barrier((own, own_other)))
    across = lax.ppermute(own, "c", SWAP)
    right_here = call(load_kernel, one(right.shape, BF), [VMEM], [], 1 << 20, 2 * channels * block_bytes)(right)
    left_other = lax.ppermute(left, "c", SWAP)
    stack = pltpu.VMEM((half, width, width), BF)
    first, message = call(
        first_kernel, [((width, width), BF), ((span, width), BF)], [SMEM, SMEM] + [VMEM] * 4,
        [pltpu.VMEM((channels, width, width), BF), pltpu.VMEM((width, channels * width), BF)],
        2 * unit, 4 * channels * block_bytes,
    )(meta, picks, own, across, left, right_here)

    message_core = lax.ppermute(message, "c", SWAP)
    message_other = lax.ppermute(message, "yh", SWAP)
    keep = call(
        keep_kernel, one((half, width, width), F32), [SMEM, VMEM, VMEM], [stack], unit, 2 * channels * block_bytes
    )(meta, message, left)
    parts = call(
        core_sum_kernel, [((2 * width + TILE, width), BF)] * 4, [SMEM] + [VMEM] * 4, [stack], unit, 3 * half * block_bytes
    )(meta, message_core, keep, left_other, message)
    arrived_x = [along_x(parts[2], 2), along_x(parts[1], 1), along_x(parts[3], 3)]
    row = call(
        row_sum_kernel, one((2 * width + TILE, width), BF), [VMEM] * 4, [], 1 << 20, 10 * block_bytes
    )(parts[0], *arrived_x)
    near, far = routes(lax.axis_size("z"), lax.axis_size("yl"))
    from_far = lax.ppermute(row, YROW, far)
    from_near = lax.ppermute(row, YROW, near)

    both = jnp.concatenate([message, message_other], axis=0)
    two_own = jnp.concatenate(round_x(both))
    two_other = lax.ppermute(two_own, "c", SWAP)
    pool_two = jnp.concatenate([two_own, two_other])
    g_send = call(
        send_kernel, one((half, width, width), BF), [SMEM, SMEM, VMEM, VMEM], [], unit // 2, channels * block_bytes
    )(meta, picks, pool_two, right_here)
    g_other = lax.ppermute(g_send, "c", SWAP)
    g_own, base = call(
        pool_two_kernel, [((half, width, width), BF), ((width, width), F32)], [SMEM, SMEM] + [VMEM] * 4, [],
        3 * unit // 2, 4 * channels * block_bytes,
    )(meta, picks, pool_two, left, right_here, g_send)

    factor = 1.0 / (width * math.sqrt(channels_of(sector_size)))
    edge = call(
        lambda *refs: edge_kernel(factor, *refs), one((2 * width, width), BF), [VMEM] * 2, [], 1 << 20, 12 * block_bytes
    )(from_near, from_far)
    edges_own = jnp.concatenate(round_x(edge))
    for_other = call(other_kernel, one((width, width), F32), [VMEM] * 2, [], unit // 2, 3 * half * block_bytes)(
        edges_own, g_other
    )
    from_other = lax.ppermute(for_other, "c", SWAP)
    from_own = call(
        own_kernel, one((width, width), F32), [SMEM] + [VMEM] * 4, [], unit // 2, 4 * half * block_bytes
    )(meta, edges_own, left, g_own, base)
    second = call(second_kernel, one((width, width), BF), [SMEM, VMEM, VMEM], [], 1 << 18, 3 * block_bytes)(
        meta, from_own, from_other
    )
    return (first[None, None], second[None, None])


def channels_of(sector_size):
    return sector_size.shape[1] * lax.axis_size(("x", "yh", "c"))


def solution(mesh):
    finer = Mesh(mesh.devices.reshape(mesh.shape["sec"] // 4, 4, 4, 2, 2), ("z", "yl", "x", "yh", "c"))
    sec, blk = ("z", "yl"), ("x", "yh", "c")
    return jax.shard_map(
        body,
        mesh=finer,
        in_specs=(
            P(sec, blk, None, None),
            P(sec, blk, None, None, None),
            P(sec, blk, None, None, None),
            P(sec, blk, None),
            P(sec, blk),
        ),
        out_specs=(P(sec, blk, None, None), P(sec, blk, None, None)),
        check_vma=False,
    )
```
